512 devices in a mesh: dp: 8 (over y_hi, core), mp: 64 (over z, x, y_lo).
Axes of the slice: x: 4, y: 8 (y_hi: 4, y_lo: 2; y = y_hi * 2 + y_lo), z: 8, core: 2. Of those that a mesh axis runs over, the one named last changes fastest.
Arguments:
- queries: bfloat16 [65536, 768], P(('dp', 'mp')), may hold values from -30 to 30
- first_owner: int32 [65536, 1], P(('dp', 'mp')), may hold values from 0 to 63; in each aligned block of 128 rows (0 to 127, 128 to 255, ...) at most 4 rows name the same one
- first_row: int32 [65536], P(('dp', 'mp')), may hold values from 0 to 255
- tool_table: bfloat16 [16384, 768], P('mp'), may hold values from -6 to 6
- norm_gain: bfloat16 [768], replicated, may hold values from 0.25 to 1.75
- weight_in: bfloat16 [3072, 768], P('mp'), may hold values from -0.21875 to 0.21875
- bias_in: bfloat16 [3072], P('mp'), may hold values from -3 to 3
- weight_out: bfloat16 [3072, 768], P('mp'), may hold values from -0.109375 to 0.109375
- bias_out: bfloat16 [768], replicated, may hold values from -3 to 3
- tool_embeds: bfloat16 [512, 768], P('dp'), may hold values from -2 to 2
- positive: int32 [65536], P(('dp', 'mp')), may hold values from 0 to 511
Outputs:
- updated: bfloat16 [65536, 768], P(('dp', 'mp'))
- chain_loss: float32 [65536], P(('dp', 'mp'))
- query_grad: float32 [65536, 768], P(('dp', 'mp'))
- tool_grad: float32 [512, 768], P('dp')
The draws below stay inside these ranges and needn't reach their ends.
Inputs may be any that keep to these rules, and one draw needn't show every extreme that they name: `first_owner`: among the 128 chains of one device at most 4 name the same owner, a bound that some block reaches of them.
All inputs are finite; a program needn't handle non-finite values.
Results may differ from the reference program's by a relative error of at most 0.0078.
Values may be sent and summed in bfloat16 or wider, within the bound.
A program may use at most 64 MiB of HBM per device.

```python
import math
import jax
import jax.numpy as jnp
import numpy as np
from jax import lax

D = 768
H = 3072
CH_DEV = 128
ROWS_OWN = 256
CAP = 4
CHAINS = 65536
TB = 512
TOOLS = 16384
N_MP = 64


def draw_queries(key, part):
    noise_key, scale_key = jax.random.split(jax.random.fold_in(key, 11))
    row_scale = jnp.exp(jax.random.uniform(scale_key, (CHAINS, 1), jnp.float32, math.log(0.5), math.log(5.0)))
    values = jnp.clip(jax.random.normal(noise_key, (CHAINS, D), jnp.float32), -6.0, 6.0) * row_scale
    return values.astype(jnp.bfloat16)


def draw_tool_embeds(key, part):
    noise_key, scale_key = jax.random.split(jax.random.fold_in(key, 23))
    row_scale = jnp.exp(jax.random.uniform(scale_key, (TB, 1), jnp.float32, math.log(0.4), math.log(4.0))) / math.sqrt(D)
    values = jnp.clip(jax.random.normal(noise_key, (TB, D), jnp.float32), -6.0, 6.0) * row_scale
    return values.astype(jnp.bfloat16)


def place_ends(values, own_key, least, largest):
    shape = values.shape
    place = [jax.random.randint(jax.random.fold_in(own_key, axis), (), 0, shape[axis]) for axis in range(len(shape))]
    values = values.at[tuple(place)].set(least)
    longest = shape.index(max(shape))
    place[longest] = (place[longest] + 1) % shape[longest]
    return values.at[tuple(place)].set(largest)


def steps_of(stream_key, shape, shards, least, largest):
    factor_of = 1.0
    for position, parts in shards:
        heights = jax.random.uniform(jax.random.fold_in(jax.random.fold_in(stream_key, 6), position), (parts,), jnp.float32, least / len(shards), largest / len(shards))
        factor_of = factor_of * jnp.repeat(jnp.exp(heights), shape[position] // parts).reshape((-1,) + (1,) * (len(shape) - 1 - position))
    return factor_of


def shared_out(rng, own, number, rows, amount, top, most, lean):
    ranking = jax.random.permutation(rng, amount)
    crowded, common = load_shares(amount, rows * top, most, lean, True), load_shares(amount, rows * top, most, lean, False)
    places = jnp.arange(amount)

    def named(lengths, offset_by):
        used = int((lengths > 0).sum())
        fixed = max(1, used // 4)
        shifted = fixed + (places - fixed + offset_by * (used - fixed)) % max(1, amount - fixed)
        return jnp.zeros((amount,), jnp.int32).at[ranking[jnp.where(places < fixed, places, shifted)]].set(jnp.asarray(lengths, jnp.int32))

    lengths = jnp.where(number % 4 == 0, named(crowded, number // 4), named(common, number - number // 4 - 1))
    mixed = jax.random.permutation(jax.random.fold_in(own, 3), amount)
    giver, receiver = mixed[0:amount // 2 * 2:2], mixed[1:amount // 2 * 2:2]
    room = jnp.minimum(lengths[giver] - 1, most - lengths[receiver]) // 2
    room = jnp.where((giver == ranking[0]) | (receiver == ranking[0]) | (lengths[receiver] == 0), 0, jnp.maximum(room, 0))
    shifted = jax.random.randint(jax.random.fold_in(own, 4), (amount // 2,), 0, 1 << 20) % (room + 1)
    lengths = lengths.at[giver].add(-shifted).at[receiver].add(shifted)
    items = jnp.searchsorted(jnp.cumsum(lengths), jnp.arange(rows * top), side="right").astype(jnp.int32)
    listing = items.reshape(top, rows).T
    listing = listing[jax.random.permutation(jax.random.fold_in(own, 1), rows)]
    offset_by = jax.random.randint(jax.random.fold_in(own, 2), (rows, 1), 0, top)
    return jnp.take_along_axis(listing, (jnp.arange(top)[None, :] + offset_by) % top, axis=1)


def load_shares(amount, total, bound, skew, full):
    loads = [(1 << 20) // math.isqrt(grade ** skew) + 1 for grade in range(1, amount + 1)]
    largest = bound if full else min(bound, max(-(-total // amount), total * loads[0] // sum(loads)))
    least = 1 if total - largest >= amount - 1 else 0
    given, rest = [largest] + [least] * (amount - 1), total - largest - least * (amount - 1)
    while rest > 0:
        candidates = [i for i in range(1, amount) if given[i] < largest] or [i for i in range(1, amount) if given[i] < bound]
        whole, remaining = sum([loads[i] for i in candidates]), rest
        for i in candidates:
            more = min(bound - given[i], max(1, remaining * loads[i] // whole), rest)
            given[i] = given[i] + more
            rest = rest - more
    return np.array(given)


def bell_draw(own_key, extent, width, most, shards=(), held_as=jnp.bfloat16):
    result = jax.random.normal(own_key, extent, jnp.float32) * width
    if len(shards) > 0:
        result = steps_of(own_key, extent, shards, -0.22, 0.18) * result
    return jnp.clip(result, min=-most, max=most).astype(held_as)


def setup_inputs(seed: int = 0) -> dict:
    keys = jax.random.split(jax.random.key(seed), 12)
    queries = draw_queries(jax.random.fold_in(keys[11], 71), 0)
    first_owner_keys = jax.random.split(jax.random.fold_in(keys[1], 1), CHAINS // CH_DEV)
    first_owner_turns = jax.random.permutation(jax.random.fold_in(keys[1], 3), CHAINS // CH_DEV)
    first_owner = jax.vmap(lambda own, number: shared_out(jax.random.fold_in(keys[1], 2), own, number, CH_DEV, N_MP, 1, CAP, 2))(first_owner_keys, first_owner_turns).reshape((CHAINS, 1))
    first_row = place_ends(jax.random.randint(keys[2], (CHAINS,), 0, ROWS_OWN), jax.random.fold_in(keys[2], 1), 0, ROWS_OWN - 1).astype(jnp.int32)
    tool_table = bell_draw(keys[3], (TOOLS, D), 1.0, 6.0, ((0, 64),))
    norm_gain = jnp.clip(1.0 + 0.15 * jax.random.normal(keys[4], (D,), jnp.float32), 0.25, 1.75).astype(jnp.bfloat16)
    weight_in = bell_draw(keys[5], (H, D), D ** -0.5, 0.21875, ((0, 64),))
    bias_in = bell_draw(keys[6], (H,), 0.5, 3.0, ((0, 64),))
    weight_out = bell_draw(keys[7], (H, D), H ** -0.5, 0.109375, ((0, 64),))
    bias_out = bell_draw(keys[8], (D,), 0.5, 3.0)
    tool_embeds = draw_tool_embeds(jax.random.fold_in(keys[11], 71), 0)
    positive = place_ends(jax.random.randint(keys[10], (CHAINS,), 0, TB), jax.random.fold_in(keys[10], 1), 0, TB - 1).astype(jnp.int32)
    return {"queries": queries, "first_owner": first_owner, "first_row": first_row, "tool_table": tool_table, "norm_gain": norm_gain, "weight_in": weight_in, "bias_in": bias_in, "weight_out": weight_out, "bias_out": bias_out, "tool_embeds": tool_embeds, "positive": positive}


def layer_normed(combined, norm_gain):
    row_mean = lax.optimization_barrier(jnp.mean(combined, axis=1, keepdims=True))
    centred = combined - row_mean
    spread = lax.optimization_barrier(jnp.mean(centred * centred, axis=1, keepdims=True))
    return (centred * lax.rsqrt(spread + 1e-05) * norm_gain.astype(jnp.float32)[None, :]).astype(jnp.bfloat16)

def reference(queries, first_owner, first_row, tool_table, norm_gain, weight_in, bias_in, weight_out, bias_out, tool_embeds, positive):
    picked = (first_owner[:, 0] * ROWS_OWN + first_row).astype(jnp.int32)
    first_rows = jnp.take(tool_table, picked, axis=0)
    combined = queries.astype(jnp.float32) + first_rows.astype(jnp.float32)
    block_count = CHAINS // CH_DEV
    tool_ids = jnp.arange(TB, dtype=jnp.int32)

    def one_block(running, inputs):
        block_comb, block_pos = inputs
        normed = layer_normed(block_comb, norm_gain)
        preact = jnp.dot(normed, weight_in.T, preferred_element_type=jnp.float32) + bias_in.astype(jnp.float32)[None, :]
        activated = jax.nn.gelu(preact, approximate=True).astype(jnp.bfloat16)
        branch_sum = jnp.dot(activated, weight_out, preferred_element_type=jnp.float32)
        updated = (block_comb + branch_sum + bias_out.astype(jnp.float32)[None, :]).astype(jnp.bfloat16)
        scores = jnp.dot(updated, tool_embeds.T, preferred_element_type=jnp.float32)
        row_max = lax.optimization_barrier(jnp.max(scores, axis=1, keepdims=True))
        log_total = row_max + jnp.log(lax.optimization_barrier(jnp.sum(jnp.exp(scores - row_max), axis=1, keepdims=True)))
        is_positive = (tool_ids[None, :] == block_pos[:, None]).astype(jnp.float32)
        chain_loss = log_total[:, 0] - lax.optimization_barrier(jnp.sum(scores * is_positive, axis=1))
        weights_grad = (jnp.exp(scores - log_total) - is_positive).astype(jnp.bfloat16)
        query_grad = jnp.dot(weights_grad, tool_embeds, preferred_element_type=jnp.float32)
        running = running + jnp.dot(weights_grad.T, updated, preferred_element_type=jnp.float32)
        return (running, (updated, chain_loss, query_grad))
    running, outputs = lax.scan(one_block, jnp.zeros((TB, D), jnp.float32), (combined.reshape(block_count, CH_DEV, D), positive.reshape(block_count, CH_DEV)))
    updated, chain_loss, query_grad = outputs
    tool_grad = running * (TB / CHAINS) ** 0.5
    return (updated.reshape(CHAINS, D), chain_loss.reshape(CHAINS), query_grad.reshape(CHAINS, D), tool_grad)
```

```python
import functools

import jax
import jax.numpy as jnp
from jax import lax
from jax.experimental import pallas as pl
from jax.experimental.pallas import tpu as pltpu
from jax.sharding import PartitionSpec as P

MESH = pl.DeviceIdType.MESH
BF, F32, I32 = jnp.bfloat16, jnp.float32, jnp.int32
NZ, NX, NYL, NYH, NC = 8, 4, 2, 4, 2
NP = NX * NYL
CAP = 4
N_SEMS = 192


def iota(shape, axis):
    return lax.broadcasted_iota(I32, shape, axis)


def bits(mask):
    return jnp.where(mask, 1.0, 0.0).astype(BF)


def dot(a, b):
    return jnp.dot(a, b, preferred_element_type=F32)


def dot_t(a, b):
    return lax.dot_general(a, b, (((1,), (1,)), ((), ())), preferred_element_type=F32)


def gelu(u):
    return 0.5 * u * (1.0 + jnp.tanh(0.7978845608028654 * (u + 0.044715 * (u * u * u))))


def kernel(
    grad_scale,
    queries,
    owner_ref,
    row_ref,
    table,
    gain,
    w_in,
    bias_in,
    w_out,
    bias_out,
    tools,
    positive,
    updated_ref,
    loss_ref,
    qgrad_ref,
    tgrad_ref,
    winb,
    woutb,
    toolsb,
    req1,
    rcv1,
    req2,
    rcv2,
    g1b,
    ra,
    bb,
    fb,
    nbuf,
    pbuf,
    rbuf,
    updb,
    wgb,
    wga,
    s1b,
    s1r,
    s2b,
    s2r,
    s3b,
    s3r,
    s4r,
    send_sems,
    recv_sems,
    local_sems,
):
    d, m = lax.axis_index("dp"), lax.axis_index("mp")
    yh, c = lax.div(d, NC), lax.rem(d, NC)
    z, p = lax.div(m, NP), lax.rem(m, NP)
    x, yl = lax.div(p, NYL), lax.rem(p, NYL)
    chains = queries.shape[0]

    def z_peer(o):
        return {"mp": lax.rem(z + o, NZ) * NP + p}

    def p_peer(o):
        return {"mp": z * NP + lax.rem(p + o, NP)}

    def x_peer(o):
        return {"mp": z * NP + lax.rem(x + o, NX) * NYL + yl}

    def y_peer(o):
        return {"dp": lax.rem(yh + o, NYH) * NC + c}

    other_core = {"dp": yh * NC + (1 - c)}
    y_flip = {"mp": z * NP + x * NYL + (1 - yl)}
    z_next = {"mp": lax.rem(z + 1 + (NZ - 2) * c, NZ) * NP + p}
    z_prev = {"mp": lax.rem(z + (NZ - 1) - (NZ - 2) * c, NZ) * NP + p}
    x_next = {"mp": z * NP + lax.rem(x + 1 + (NX - 2) * c, NX) * NYL + yl}
    x_prev = {"mp": z * NP + lax.rem(x + (NX - 1) - (NX - 2) * c, NX) * NYL + yl}

    def zb(k):
        return lax.rem(z - k + 2 * k * c + NZ, NZ)

    def xb(k):
        return lax.rem(x - k + 2 * k * c + NX, NX)

    count = [0]
    started = []

    def remote(src, dst, peer):
        i = count[0]
        count[0] += 1
        return pltpu.make_async_remote_copy(
            src_ref=src,
            dst_ref=dst,
            send_sem=send_sems.at[i],
            recv_sem=recv_sems.at[i],
            device_id=peer,
            device_id_type=MESH,
        )

    def send(src, dst, peer):
        copy = remote(src, dst, peer)
        copy.start()
        started.append(copy)
        return copy

    def arrive(copies):
        for copy in copies:
            copy.wait_recv()

    barrier = pltpu.get_barrier_semaphore()
    peers = [z_peer(o) for o in range(1, NZ)] + [p_peer(o) for o in range(1, NP)]
    peers += [y_peer(o) for o in range(1, NYH)] + [other_core]
    for peer in peers:
        pl.semaphore_signal(barrier, inc=1, device_id=peer, device_id_type=MESH)
    pl.semaphore_wait(barrier, len(peers))

    y_in = remote(w_in, winb.at[z, x], y_flip)
    y_out = remote(w_out, woutb.at[z, x], y_flip)
    own_in = pltpu.make_async_copy(w_in, winb.at[z, x], local_sems.at[0])
    own_out = pltpu.make_async_copy(w_out, woutb.at[z, x], local_sems.at[1])

    @pl.when(c == yl)
    def _():
        y_in.start()
        y_out.start()
        own_in.start()
        own_out.start()

    own_tools = pltpu.make_async_copy(tools, toolsb.at[c * NYH + yh], local_sems.at[2])
    own_tools.start()
    tool_sends = [send(tools, toolsb.at[c * NYH + yh], y_peer(o)) for o in range(1, NYH)]
    tool_swaps = [send(tools, toolsb.at[c * NYH + yh], other_core)]

    owner = owner_ref[...]
    eye = iota((chains, chains), 0) == iota((chains, chains), 1)
    own_mask = owner == iota((chains, NZ * NP), 1)
    earlier = bits(iota((chains, chains), 1) < iota((chains, chains), 0))
    prior = dot(earlier, bits(own_mask))
    rank = jnp.sum(jnp.where(own_mask, prior, 0.0), axis=1, keepdims=True).astype(I32)
    row_col = jnp.sum(jnp.where(eye, row_ref[...].astype(F32), 0.0), axis=1, keepdims=True)
    owner_row = jnp.sum(jnp.where(eye, owner.astype(F32), 0.0), axis=0, keepdims=True).astype(I32)
    lane_of = (owner & (NP - 1)) * CAP + rank
    spread = jnp.where(iota((chains, 128), 1) == lane_of, row_col, 0.0).astype(BF)
    to_z = bits((owner_row >> 3) == iota((16, chains), 0))
    bias_line = jnp.where(iota((16, 128), 0) == NZ, bias_in[...].astype(F32), 0.0)
    req1[...] = dot(to_z, spread) + bias_line
    rcv1[z] = req1[...]
    reqs1 = [send(req1, rcv1.at[z], z_peer(o)) for o in range(1, NZ)]

    @pl.when(c == yl)
    def _():
        own_in.wait()
        own_out.wait()

    @pl.when(c != yl)
    def _():
        y_in.wait_recv()
        y_out.wait_recv()

    a_x = {NX - o: send(winb.at[z, x], winb.at[z, x], x_peer(o)) for o in range(1, NX)}
    a_next, a_prev, b_next, b_prev, b_x = {}, {}, {}, {}, {}

    def a_step(k, j):
        xj = lax.rem(x + j, NX)
        if k == 1 and j > 0:
            a_x[j].wait_recv()
        if k > 1:
            a_next[k - 1, j].wait_recv()
        src = winb.at[zb(k - 1), xj]
        a_next[k, j] = send(src, src, z_next)
        if k <= 3:
            if k > 1:
                a_prev[k - 1, j].wait_recv()
            src = winb.at[zb(1 - k), xj]
            a_prev[k, j] = send(src, src, z_prev)

    def b_cross(k):
        src = woutb.at[zb(k), x]
        b_x[k, 1] = send(src, src, x_next)
        b_x[k, -1] = send(src, src, x_prev)

    def b_relay(k):
        b_x[k, 1].wait_recv()
        src = woutb.at[zb(k), xb(1)]
        b_x[k, 2] = send(src, src, x_next)

    def b_step(k):
        if k > 1:
            b_next[k - 1].wait_recv()
        src = woutb.at[zb(k - 1), x]
        b_next[k] = send(src, src, z_next)
        if k <= 3:
            if k > 1:
                b_prev[k - 1].wait_recv()
            src = woutb.at[zb(1 - k), x]
            b_prev[k] = send(src, src, z_prev)

    a_step(1, 0)
    b_step(1)
    b_cross(0)

    arrive(reqs1)
    for zz in range(NZ):
        tile = rcv1[zz]
        mine = jnp.where(iota((16, 128), 0) == z, tile, 0.0)
        req2[zz : zz + 1, :] = jnp.sum(mine, axis=0, keepdims=True)
        req2[NZ + zz : NZ + zz + 1, :] = tile[NZ : NZ + 1, :]
    rcv2[p] = req2[...]
    reqs2 = [send(req2, rcv2.at[p], p_peer(o)) for o in range(1, NP)]

    for j in range(1, NX):
        a_step(1, j)
    b_step(2)
    b_cross(1)
    b_cross(-1)
    b_relay(0)

    arrive(reqs2)
    asked = jnp.concatenate([rcv2[pp, 0:NZ, :] for pp in range(NP)], axis=0).astype(BF)
    slots = NZ * NP * CAP
    thrice = dot(bits((iota((slots, NZ * NP), 0) >> 2) == iota((slots, NZ * NP), 1)), asked)
    lane_mine = iota((slots, 128), 1) == (iota((slots, 128), 0) & (CAP - 1)) + CAP * p
    wanted = jnp.sum(jnp.where(lane_mine, thrice, 0.0), axis=1, keepdims=True).astype(I32)
    pick = bits(wanted == iota((slots, table.shape[0]), 1))
    g1b[...] = dot(pick, table[...]).astype(BF).reshape(g1b.shape)
    ra[p] = g1b[p]
    rows1 = [send(g1b.at[lax.rem(p + o, NP)], ra.at[p], p_peer(o)) for o in range(1, NP)]

    for j in range(NX):
        a_step(2, j)
    b_step(3)
    b_cross(2)
    b_cross(-2)
    b_relay(1)
    b_relay(-1)

    arrive(rows1)
    i0 = iota((slots, slots), 0)
    order1 = ((i0 >> 2) & (NP - 1)) * 32 + (i0 >> 5) * CAP + (i0 & (CAP - 1))
    regrouped = dot(bits(order1 == iota((slots, slots), 1)), ra[...].reshape(slots, -1))
    bb[...] = regrouped.astype(BF).reshape(bb.shape)
    fb[z] = bb[z]
    rows2 = [send(bb.at[lax.rem(z + o, NZ)], fb.at[z], z_peer(o)) for o in range(1, NZ)]

    for j in range(NX):
        a_step(3, j)
    b_step(4)
    b_prev[3].wait_recv()
    b_cross(3)
    b_cross(-3)
    b_relay(2)
    b_relay(-2)
    arrive(tool_sends)
    for o in range(1, NYH):
        slot = toolsb.at[c * NYH + lax.rem(yh + o, NYH)]
        tool_swaps.append(send(slot, slot, other_core))

    arrive(rows2)
    select = bits(owner * CAP + rank == iota((chains, slots), 1))
    combined = queries[...].astype(F32) + dot(select, fb[...].reshape(slots, -1))
    centred = combined - jnp.mean(combined, axis=1, keepdims=True)
    spread_sq = jnp.mean(centred * centred, axis=1, keepdims=True)
    normed = centred * lax.rsqrt(spread_sq + 1e-05) * gain[...].astype(F32)
    nbuf[c] = normed.astype(BF)
    swap_n = send(nbuf.at[c], nbuf.at[c], other_core)

    for j in range(NX):
        a_step(4, j)
    b_next[4].wait_recv()
    b_cross(4)
    b_relay(3)
    b_relay(-3)
    b_relay(4)

    units = w_in.shape[0]
    hidden = NZ * NX * units
    bias_rows = jnp.concatenate([rcv2[NYL * xx + c, NZ : 2 * NZ, :] for xx in range(NX)], axis=0)
    lane = iota((128, hidden), 1)
    spread_bias = dot(bias_rows.astype(BF), bits(iota((128, hidden), 0) == lane - units * ((lane * 1366) >> 16)))
    shard = (iota((NX * NZ, hidden), 1) * 1366) >> 16
    shard_row = (shard & (NX - 1)) * NZ + (shard >> 2)
    bias_row = jnp.sum(jnp.where(shard_row == iota((NX * NZ, hidden), 0), spread_bias, 0.0), axis=0, keepdims=True)

    swap_n.wait_recv()
    for j in range(NX):
        a_prev[3, j].wait_recv()
        a_next[4, j].wait_recv()
    for k in (0, 1, -1, 2, -2, 3, -3, 4):
        b_x[k, -1].wait_recv()
        b_x[k, 2].wait_recv()

    both = nbuf[...].reshape(2 * chains, -1)
    group = 2
    width = group * NX * units
    branch = None
    for g in range(NZ // group):
        block = winb[g * group : (g + 1) * group].reshape(width, -1)
        act = gelu(dot_t(both, block) + bias_row[:, g * width : (g + 1) * width]).astype(BF)
        term = dot(act, woutb[g * group : (g + 1) * group].reshape(width, -1))
        branch = term if branch is None else branch + term
    pbuf[...] = branch.reshape(pbuf.shape)
    swap_p = send(pbuf.at[1 - c], rbuf, other_core)
    swap_p.wait_recv()
    updated = (combined + (pbuf[c] + rbuf[...]) + bias_out[...].astype(F32)).astype(BF)
    updated_ref[...] = updated
    updb[c] = updated
    swap_u = send(updb.at[c], updb.at[c], other_core)

    arrive(tool_swaps)
    own_tools.wait()
    all_tools = toolsb[...].reshape(NC * NYH * tools.shape[0], -1)
    n_tools = all_tools.shape[0]
    half = n_tools // 2
    scores = dot_t(updated, all_tools)
    pos = jnp.sum(jnp.where(eye, positive[...].astype(F32), 0.0), axis=1, keepdims=True).astype(I32)
    pos_col = ((pos >> 6) & 1) * half + (pos >> 7) * 64 + (pos & 63)
    is_pos = iota((chains, n_tools), 1) == pos_col
    top = jnp.max(scores, axis=1, keepdims=True)
    log_total = top + jnp.log(jnp.sum(jnp.exp(scores - top), axis=1, keepdims=True))
    loss = log_total - jnp.sum(jnp.where(is_pos, scores, 0.0), axis=1, keepdims=True)
    grad = (jnp.exp(scores - log_total) - jnp.where(is_pos, 1.0, 0.0)).astype(BF)
    wgb[0] = grad[:, :half]
    wgb[1] = grad[:, half:]
    swap_w = send(wgb.at[1 - c], wga.at[c], other_core)
    wga[c] = wgb[c]
    loss_ref[...] = jnp.sum(jnp.where(eye, loss, 0.0), axis=0, keepdims=True)
    qgrad_ref[...] = dot(grad, all_tools)

    arrive([swap_u, swap_w])
    i1 = iota((half, half), 0)
    order2 = ((i1 >> 3) & (NYH - 1)) * 64 + (i1 >> 5) * 8 + (i1 & 7)
    grad_t = dot_t(bits(order2 == iota((half, half), 1)), wga[...].reshape(2 * chains, half)).astype(BF)
    part = dot(grad_t, updb[...].reshape(2 * chains, -1))
    s1b[...] = part.astype(BF).reshape(s1b.shape)
    s1r[p] = s1b[p]
    arrive([send(s1b.at[lax.rem(p + o, NP)], s1r.at[p], p_peer(o)) for o in range(1, NP)])
    total = s1r[0].astype(F32)
    for i in range(1, NP):
        total = total + s1r[i].astype(F32)
    s2b[...] = total.reshape(s2b.shape)
    s2r[yh] = s2b[yh]
    arrive([send(s2b.at[lax.rem(yh + o, NYH)], s2r.at[yh], y_peer(o)) for o in range(1, NYH)])
    total = s2r[0]
    for i in range(1, NYH):
        total = total + s2r[i]
    s3b[...] = total
    s3r[z] = total
    arrive([send(s3b, s3r.at[z], z_peer(o)) for o in range(1, NZ)])
    total = s3r[0]
    for i in range(1, NZ):
        total = total + s3r[i]
    s4r[p] = total * grad_scale
    arrive([send(s4r.at[p], s4r.at[p], p_peer(o)) for o in range(1, NP)])
    tgrad_ref[...] = s4r[...].reshape(tgrad_ref.shape)

    for copy in started:
        copy.wait_send()

    @pl.when(c == yl)
    def _():
        y_in.wait_send()
        y_out.wait_send()


def solution(mesh):
    def local(queries, owner, row, table, gain, w_in, bias_in, w_out, bias_out, tools, positive):
        n, feat = queries.shape
        units = w_in.shape[0]
        block = tools.shape[0]
        scale = (block * mesh.shape["dp"] / (n * mesh.shape["dp"] * mesh.shape["mp"])) ** 0.5
        vmem = pl.BlockSpec(memory_space=pltpu.VMEM)
        slot_rows = NP * CAP
        sub = block // NP
        scratch = [
            pltpu.VMEM((NZ, NX, units, feat), BF),
            pltpu.VMEM((NZ, NX, units, feat), BF),
            pltpu.VMEM((NC * NYH, block, feat), BF),
            pltpu.VMEM((16, 128), F32),
            pltpu.VMEM((NZ, 16, 128), F32),
            pltpu.VMEM((16, 128), F32),
            pltpu.VMEM((NP, 16, 128), F32),
            pltpu.VMEM((NP, slot_rows, feat), BF),
            pltpu.VMEM((NP, slot_rows, feat), BF),
            pltpu.VMEM((NZ, slot_rows, feat), BF),
            pltpu.VMEM((NZ, slot_rows, feat), BF),
            pltpu.VMEM((NC, n, feat), BF),
            pltpu.VMEM((NC, n, feat), F32),
            pltpu.VMEM((n, feat), F32),
            pltpu.VMEM((NC, n, feat), BF),
            pltpu.VMEM((NC, n, NYH * block), BF),
            pltpu.VMEM((NC, n, NYH * block), BF),
            pltpu.VMEM((NP, NYH * sub, feat), BF),
            pltpu.VMEM((NP, NYH * sub, feat), BF),
            pltpu.VMEM((NYH, sub, feat), F32),
            pltpu.VMEM((NYH, sub, feat), F32),
            pltpu.VMEM((sub, feat), F32),
            pltpu.VMEM((NZ, sub, feat), F32),
            pltpu.VMEM((NP, sub, feat), F32),
            pltpu.SemaphoreType.DMA((N_SEMS,)),
            pltpu.SemaphoreType.DMA((N_SEMS,)),
            pltpu.SemaphoreType.DMA((3,)),
        ]
        updated, loss, qgrad, tgrad = pl.pallas_call(
            functools.partial(kernel, scale),
            out_shape=(
                jax.ShapeDtypeStruct((n, feat), BF),
                jax.ShapeDtypeStruct((1, n), F32),
                jax.ShapeDtypeStruct((n, feat), F32),
                jax.ShapeDtypeStruct((block, feat), F32),
            ),
            in_specs=[vmem] * 11,
            out_specs=(vmem,) * 4,
            scratch_shapes=scratch,
            compiler_params=pltpu.CompilerParams(
                collective_id=0, has_side_effects=True, vmem_limit_bytes=48 << 20
            ),
        )(
            queries,
            owner,
            row.reshape(1, n),
            table,
            gain.reshape(1, feat),
            w_in,
            jnp.pad(bias_in.reshape(1, units), ((0, 0), (0, 128 - units))),
            w_out,
            bias_out.reshape(1, feat),
            tools,
            positive.reshape(1, n),
        )
        return updated, loss.reshape(n), qgrad, tgrad

    in_specs = (
        P(("dp", "mp"), None),
        P(("dp", "mp"), None),
        P(("dp", "mp")),
        P("mp", None),
        P(),
        P("mp", None),
        P("mp"),
        P("mp", None),
        P(),
        P("dp", None),
        P(("dp", "mp")),
    )
    out_specs = (P(("dp", "mp"), None), P(("dp", "mp")), P(("dp", "mp"), None), P("dp", None))
    return jax.shard_map(local, mesh=mesh, in_specs=in_specs, out_specs=out_specs, check_vma=False)
```

```python
import functools

import jax
import jax.numpy as jnp
from jax import lax
from jax.experimental import pallas as pl
from jax.experimental.pallas import tpu as pltpu
from jax.sharding import PartitionSpec as P

MESH = pl.DeviceIdType.MESH
BF, F32, I32 = jnp.bfloat16, jnp.float32, jnp.int32
NZ, NX, NYL, NYH, NC = 8, 4, 2, 4, 2
NP = NX * NYL
CAP = 4
N_SEMS = 192


def iota(shape, axis):
    return lax.broadcasted_iota(I32, shape, axis)


def bits(mask):
    return jnp.where(mask, 1.0, 0.0).astype(BF)


def dot(a, b):
    return jnp.dot(a, b, preferred_element_type=F32)


def dot_t(a, b):
    return lax.dot_general(a, b, (((1,), (1,)), ((), ())), preferred_element_type=F32)


def gelu(u):
    return 0.5 * u * (1.0 + jnp.tanh(0.7978845608028654 * (u + 0.044715 * (u * u * u))))


def kernel(
    grad_scale,
    queries_hbm,
    owner_hbm,
    row_hbm,
    positive_hbm,
    table_hbm,
    w_in,
    w_out,
    tools,
    gain_hbm,
    bias_out_hbm,
    bias_in_hbm,
    updated_ref,
    loss_ref,
    qgrad_ref,
    tgrad_ref,
    queries,
    owner_ref,
    row_ref,
    positive,
    table,
    gain_ref,
    bias_out_ref,
    bias_in_ref,
    bias_mat,
    wb,
    toolsb,
    req1,
    rcv1,
    req2,
    rcv2,
    g1b,
    ra,
    bb,
    fb,
    nbuf,
    pbuf,
    rbuf,
    updb,
    wgb,
    wga,
    s1b,
    s1r,
    s2b,
    s2r,
    s3b,
    s3r,
    s4r,
    send_sems,
    recv_sems,
    local_sems,
):
    d, m = lax.axis_index("dp"), lax.axis_index("mp")
    yh, c = lax.div(d, NC), lax.rem(d, NC)
    z, p = lax.div(m, NP), lax.rem(m, NP)
    x, yl = lax.div(p, NYL), lax.rem(p, NYL)
    chains, feat = queries.shape
    units = w_in.shape[0]
    split = 2 * units // 3

    def z_peer(o):
        return {"mp": lax.rem(z + o, NZ) * NP + p}

    def p_peer(o):
        return {"mp": z * NP + lax.rem(p + o, NP)}

    def x_peer(o):
        return {"mp": z * NP + lax.rem(x + o, NX) * NYL + yl}

    def y_peer(o):
        return {"dp": lax.rem(yh + o, NYH) * NC + c}

    other_core = {"dp": yh * NC + (1 - c)}
    y_flip = {"mp": z * NP + x * NYL + (1 - yl)}
    z_next = {"mp": lax.rem(z + 1 + (NZ - 2) * c, NZ) * NP + p}
    z_prev = {"mp": lax.rem(z + (NZ - 1) - (NZ - 2) * c, NZ) * NP + p}
    x_next = {"mp": z * NP + lax.rem(x + 1 + (NX - 2) * c, NX) * NYL + yl}
    x_prev = {"mp": z * NP + lax.rem(x + (NX - 1) - (NX - 2) * c, NX) * NYL + yl}

    def zb(k):
        return lax.rem(z - k + 2 * k * c + NZ, NZ)

    def xb(k):
        return lax.rem(x - k + 2 * k * c + NX, NX)

    count = [0]
    started = []
    arrived = set()

    def remote(src, dst, peer):
        i = count[0]
        count[0] += 1
        return pltpu.make_async_remote_copy(
            src_ref=src,
            dst_ref=dst,
            send_sem=send_sems.at[i],
            recv_sem=recv_sems.at[i],
            device_id=peer,
            device_id_type=MESH,
        )

    def send(src, dst, peer):
        copy = remote(src, dst, peer)
        copy.start()
        started.append(copy)
        return copy

    def arrive(copies):
        for copy in copies:
            if id(copy) not in arrived:
                arrived.add(id(copy))
                copy.wait_recv()

    barrier = pltpu.get_barrier_semaphore()
    peers = [z_peer(o) for o in range(1, NZ)] + [p_peer(o) for o in range(1, NP)]
    peers += [y_peer(o) for o in range(1, NYH)] + [other_core]
    for peer in peers:
        pl.semaphore_signal(barrier, inc=1, device_id=peer, device_id_type=MESH)

    def load(src, dst, i):
        copy = pltpu.make_async_copy(src, dst, local_sems.at[i])
        copy.start()
        return copy

    smalls = [
        (owner_hbm, owner_ref),
        (row_hbm, row_ref),
        (positive_hbm, positive),
        (gain_hbm, gain_ref),
        (bias_out_hbm, bias_out_ref),
        (bias_in_hbm, bias_in_ref),
    ]
    small_loads = [load(src, dst, 7 + i) for i, (src, dst) in enumerate(smalls)]
    table_load = load(table_hbm, table, 2)
    queries_load = load(queries_hbm, queries, 3)
    own_tools = load(tools, toolsb.at[c * NYH + yh], 4)
    for copy in small_loads:
        copy.wait()
    gain = gain_ref[...].astype(F32).reshape(1, feat)
    bias_out = bias_out_ref[...].astype(F32).reshape(1, feat)
    bias_in = jnp.pad(bias_in_ref[...].astype(F32).reshape(1, units), ((0, 0), (0, 128 - units)))

    eye = iota((chains, chains), 0) == iota((chains, chains), 1)
    owner_row = owner_ref[...]
    owner = jnp.sum(jnp.where(eye, owner_row.astype(F32), 0.0), axis=1, keepdims=True).astype(I32)
    own_mask = owner == iota((chains, NZ * NP), 1)
    earlier = bits(iota((chains, chains), 1) < iota((chains, chains), 0))
    prior = dot(earlier, bits(own_mask))
    rank = jnp.sum(jnp.where(own_mask, prior, 0.0), axis=1, keepdims=True).astype(I32)
    row_col = jnp.sum(jnp.where(eye, row_ref[...].astype(F32), 0.0), axis=1, keepdims=True)
    lane_of = (owner & (NP - 1)) * CAP + rank
    spread = jnp.where(iota((chains, 128), 1) == lane_of, row_col, 0.0).astype(BF)
    to_z = bits((owner_row >> 3) == iota((16, chains), 0))
    bias_line = jnp.where(iota((16, 128), 0) == NZ, bias_in, 0.0)
    req1[...] = dot(to_z, spread) + bias_line
    rcv1[z] = req1[...]
    pl.semaphore_wait(barrier, len(peers))
    reqs1 = [send(req1, rcv1.at[z], z_peer(o)) for o in range(1, NZ)]

    in_slot, out_slot = wb.at[z, x, 0:units], wb.at[z, x, units : 2 * units]
    y_in = remote(w_in, in_slot, y_flip)
    y_out = remote(w_out, out_slot, y_flip)
    own_in = pltpu.make_async_copy(w_in, in_slot, local_sems.at[5])
    own_out = pltpu.make_async_copy(w_out, out_slot, local_sems.at[6])

    @pl.when(c == yl)
    def _():
        y_in.start()
        y_out.start()
        own_in.start()
        own_out.start()

    @pl.when(c == yl)
    def _():
        own_in.wait()
        own_out.wait()

    @pl.when(c != yl)
    def _():
        y_in.wait_recv()
        y_out.wait_recv()

    def a_part(zz, xx):
        return wb.at[zz, xx, 0:split]

    def b_part(zz, xx):
        return wb.at[zz, xx, split : 2 * units]

    a_x = {NX - o: send(a_part(z, x), a_part(z, x), x_peer(o)) for o in range(1, NX)}
    a_next, a_prev, b_next, b_prev, b_x = {}, {}, {}, {}, {}

    def a_step(k, j):
        xj = lax.rem(x + j, NX)
        if k == 1 and j > 0:
            arrive([a_x[j]])
        if k > 1:
            arrive([a_next[k - 1, j]])
        src = a_part(zb(k - 1), xj)
        a_next[k, j] = send(src, src, z_next)
        if k <= 3:
            if k > 1:
                arrive([a_prev[k - 1, j]])
            src = a_part(zb(1 - k), xj)
            a_prev[k, j] = send(src, src, z_prev)

    def b_cross(k):
        if k:
            arrive([b_next[k] if k > 0 else b_prev[-k]])
        src = b_part(zb(k), x)
        b_x[k, 1] = send(src, src, x_next)
        b_x[k, -1] = send(src, src, x_prev)

    def b_relay(k):
        arrive([b_x[k, 1]])
        src = b_part(zb(k), xb(1))
        b_x[k, 2] = send(src, src, x_next)

    def b_step(k):
        if k > 1:
            arrive([b_next[k - 1]])
        src = b_part(zb(k - 1), x)
        b_next[k] = send(src, src, z_next)
        if k <= 3:
            if k > 1:
                arrive([b_prev[k - 1]])
            src = b_part(zb(1 - k), x)
            b_prev[k] = send(src, src, z_prev)

    b_step(1)
    a_step(1, 0)
    b_cross(0)

    arrive(reqs1)
    for zz in range(NZ):
        tile = rcv1[zz]
        mine = jnp.where(iota((16, 128), 0) == z, tile, 0.0)
        req2[zz : zz + 1, :] = jnp.sum(mine, axis=0, keepdims=True)
        req2[NZ + zz : NZ + zz + 1, :] = tile[NZ : NZ + 1, :]
    rcv2[p] = req2[...]
    reqs2 = [send(req2, rcv2.at[p], p_peer(o)) for o in range(1, NP)]

    b_step(2)
    b_cross(1)
    b_cross(-1)
    for j in range(1, NX):
        a_step(1, j)
    b_relay(0)

    arrive(reqs2)
    table_load.wait()
    asked = jnp.concatenate([rcv2[pp, 0:NZ, :] for pp in range(NP)], axis=0).astype(BF)
    slots = NZ * NP * CAP
    thrice = dot(bits((iota((slots, NZ * NP), 0) >> 2) == iota((slots, NZ * NP), 1)), asked)
    lane_mine = iota((slots, 128), 1) == (iota((slots, 128), 0) & (CAP - 1)) + CAP * p
    wanted = jnp.sum(jnp.where(lane_mine, thrice, 0.0), axis=1, keepdims=True).astype(I32)
    pick = bits(wanted == iota((slots, table.shape[0]), 1))
    g1b[...] = dot(pick, table[...]).astype(BF).reshape(g1b.shape)
    ra[p] = g1b[p]
    rows1 = [send(g1b.at[lax.rem(p + o, NP)], ra.at[p], p_peer(o)) for o in range(1, NP)]

    b_step(3)
    b_cross(2)
    b_cross(-2)
    a_step(2, 0)
    a_step(2, 1)
    b_relay(1)
    b_relay(-1)

    arrive(rows1)
    i0 = iota((slots, slots), 0)
    order1 = ((i0 >> 2) & (NP - 1)) * 32 + (i0 >> 5) * CAP + (i0 & (CAP - 1))
    regrouped = dot(bits(order1 == iota((slots, slots), 1)), ra[...].reshape(slots, -1))
    bb[...] = regrouped.astype(BF).reshape(bb.shape)
    fb[z] = bb[z]
    tool_sends = [send(tools, toolsb.at[c * NYH + yh], y_peer(o)) for o in range(1, NYH)]
    tool_swaps = [send(tools, toolsb.at[c * NYH + yh], other_core)]
    rows2 = [send(bb.at[lax.rem(z + o, NZ)], fb.at[z], z_peer(o)) for o in range(1, NZ)]

    b_step(4)
    b_cross(3)
    b_cross(-3)
    a_step(2, 2)
    a_step(2, 3)
    b_relay(2)
    b_relay(-2)
    b_cross(4)
    a_step(3, 0)
    a_step(3, 1)
    b_relay(3)
    b_relay(-3)

    width = NX * units
    bias_rows = jnp.concatenate([rcv2[NYL * xx + c, NZ : 2 * NZ, :] for xx in range(NX)], axis=1)
    line = iota((NX * 128, width), 0)
    lane_to = bits(((line & 127) < units) & (iota((NX * 128, width), 1) == (line >> 7) * units + (line & 127)))
    bias_mat[...] = dot(bias_rows.astype(BF), lane_to)
    queries_load.wait()

    arrive(rows2)
    select = bits(owner * CAP + rank == iota((chains, slots), 1))
    combined = queries[...].astype(F32) + dot(select, fb[...].reshape(slots, -1))
    centred = combined - jnp.mean(combined, axis=1, keepdims=True)
    spread_sq = jnp.mean(centred * centred, axis=1, keepdims=True)
    normed = centred * lax.rsqrt(spread_sq + 1e-05) * gain
    nbuf[c] = normed.astype(BF)
    swap_n = send(nbuf.at[c], nbuf.at[c], other_core)

    a_step(3, 2)
    a_step(3, 3)
    b_relay(4)

    arrive([swap_n])
    both = nbuf[...].reshape(2 * chains, feat)

    def hidden(k):
        if k:
            arrive([(a_next if k > 0 else a_prev)[abs(k), j] for j in range(NX)])
        arrive([b_x[k, -1], b_x[k, 2]])
        zz = zb(k)
        pre = dot_t(both, wb[zz, :, 0:units].reshape(width, feat)) + bias_mat[pl.ds(zz, 1), :]
        term = dot(gelu(pre).astype(BF), wb[zz, :, units : 2 * units].reshape(width, feat)).reshape(pbuf.shape)
        pbuf[...] = term if k == 0 else pbuf[...] + term

    hidden(0)
    for j in range(NX):
        a_step(4, j)
    arrive(tool_sends)
    for o in range(1, NYH):
        slot = toolsb.at[c * NYH + lax.rem(yh + o, NYH)]
        tool_swaps.append(send(slot, slot, other_core))
    for k in (1, -1, 2, -2, 3, -3, 4):
        hidden(k)
    swap_p = send(pbuf.at[1 - c], rbuf, other_core)
    arrive([swap_p])
    updated = (combined + (pbuf[c] + rbuf[...]) + bias_out).astype(BF)
    updated_ref[...] = updated
    updb[c] = updated
    swap_u = send(updb.at[c], updb.at[c], other_core)

    arrive(tool_swaps)
    own_tools.wait()
    all_tools = toolsb[...].reshape(NC * NYH * tools.shape[0], -1)
    n_tools = all_tools.shape[0]
    half = n_tools // 2
    scores = dot_t(updated, all_tools)
    pos = jnp.sum(jnp.where(eye, positive[...].astype(F32), 0.0), axis=1, keepdims=True).astype(I32)
    pos_col = ((pos >> 6) & 1) * half + (pos >> 7) * 64 + (pos & 63)
    is_pos = iota((chains, n_tools), 1) == pos_col
    top = jnp.max(scores, axis=1, keepdims=True)
    log_total = top + jnp.log(jnp.sum(jnp.exp(scores - top), axis=1, keepdims=True))
    loss = log_total - jnp.sum(jnp.where(is_pos, scores, 0.0), axis=1, keepdims=True)
    grad = (jnp.exp(scores - log_total) - jnp.where(is_pos, 1.0, 0.0)).astype(BF)
    wgb[0] = grad[:, :half]
    wgb[1] = grad[:, half:]
    swap_w = send(wgb.at[1 - c], wga.at[c], other_core)
    wga[c] = wgb[c]

    arrive([swap_u, swap_w])
    i1 = iota((half, half), 0)
    order2 = ((i1 >> 3) & (NYH - 1)) * 64 + (i1 >> 5) * 8 + (i1 & 7)
    grad_t = dot_t(bits(order2 == iota((half, half), 1)), wga[...].reshape(2 * chains, half)).astype(BF)
    part = dot(grad_t, updb[...].reshape(2 * chains, -1))
    s1b[...] = part.astype(BF).reshape(s1b.shape)
    s1r[p] = s1b[p]
    stage1 = [send(s1b.at[lax.rem(p + o, NP)], s1r.at[p], p_peer(o)) for o in range(1, NP)]
    loss_ref[...] = jnp.sum(jnp.where(eye, loss, 0.0), axis=0, keepdims=True)
    qgrad_ref[...] = dot(grad, all_tools)
    arrive(stage1)
    total = s1r[0].astype(F32)
    for i in range(1, NP):
        total = total + s1r[i].astype(F32)
    s2b[...] = total.reshape(s2b.shape).astype(BF)
    s2r[yh] = s2b[yh]
    arrive([send(s2b.at[lax.rem(yh + o, NYH)], s2r.at[yh], y_peer(o)) for o in range(1, NYH)])
    total = s2r[0].astype(F32)
    for i in range(1, NYH):
        total = total + s2r[i].astype(F32)
    s3b[...] = total.astype(BF)
    s3r[z] = s3b[...]
    arrive([send(s3b, s3r.at[z], z_peer(o)) for o in range(1, NZ)])
    total = s3r[0].astype(F32)
    for i in range(1, NZ):
        total = total + s3r[i].astype(F32)
    s4r[p] = (total * grad_scale).astype(BF)
    arrive([send(s4r.at[p], s4r.at[p], p_peer(o)) for o in range(1, NP)])
    tgrad_ref[...] = s4r[...].astype(F32).reshape(tgrad_ref.shape)

    for copy in started:
        copy.wait_send()

    @pl.when(c == yl)
    def _():
        y_in.wait_send()
        y_out.wait_send()


def hand_over(*refs):
    sems = refs[8]
    copies = [pltpu.make_async_copy(refs[i], refs[4 + i], sems.at[i]) for i in range(4)]
    for copy in copies:
        copy.start()
    for copy in copies:
        copy.wait()


def solution(mesh):
    def local(queries, owner, row, table, gain, w_in, bias_in, w_out, bias_out, tools, positive):
        n, feat = queries.shape
        units = w_in.shape[0]
        block = tools.shape[0]
        scale = (block * mesh.shape["dp"] / (n * mesh.shape["dp"] * mesh.shape["mp"])) ** 0.5
        vmem = pl.BlockSpec(memory_space=pltpu.VMEM)
        slot_rows = NP * CAP
        sub = block // NP
        scratch = [
            pltpu.VMEM((n, feat), BF),
            pltpu.VMEM((1, n), I32),
            pltpu.VMEM((1, n), I32),
            pltpu.VMEM((1, n), I32),
            pltpu.VMEM(table.shape, BF),
            pltpu.VMEM((feat,), BF),
            pltpu.VMEM((feat,), BF),
            pltpu.VMEM((units,), BF),
            pltpu.VMEM((NZ, NX * units), F32),
            pltpu.VMEM((NZ, NX, 2 * units, feat), BF),
            pltpu.VMEM((NC * NYH, block, feat), BF),
            pltpu.VMEM((16, 128), F32),
            pltpu.VMEM((NZ, 16, 128), F32),
            pltpu.VMEM((16, 128), F32),
            pltpu.VMEM((NP, 16, 128), F32),
            pltpu.VMEM((NP, slot_rows, feat), BF),
            pltpu.VMEM((NP, slot_rows, feat), BF),
            pltpu.VMEM((NZ, slot_rows, feat), BF),
            pltpu.VMEM((NZ, slot_rows, feat), BF),
            pltpu.VMEM((NC, n, feat), BF),
            pltpu.VMEM((NC, n, feat), F32),
            pltpu.VMEM((n, feat), F32),
            pltpu.VMEM((NC, n, feat), BF),
            pltpu.VMEM((NC, n, NYH * block), BF),
            pltpu.VMEM((NC, n, NYH * block), BF),
            pltpu.VMEM((NP, NYH * sub, feat), BF),
            pltpu.VMEM((NP, NYH * sub, feat), BF),
            pltpu.VMEM((NYH, sub, feat), BF),
            pltpu.VMEM((NYH, sub, feat), BF),
            pltpu.VMEM((sub, feat), BF),
            pltpu.VMEM((NZ, sub, feat), BF),
            pltpu.VMEM((NP, sub, feat), BF),
            pltpu.SemaphoreType.DMA((N_SEMS,)),
            pltpu.SemaphoreType.DMA((N_SEMS,)),
            pltpu.SemaphoreType.DMA((13,)),
        ]
        updated, loss, qgrad, tgrad = pl.pallas_call(
            functools.partial(kernel, scale),
            out_shape=(
                jax.ShapeDtypeStruct((n, feat), BF),
                jax.ShapeDtypeStruct((1, n), F32),
                jax.ShapeDtypeStruct((n, feat), F32),
                jax.ShapeDtypeStruct((block, feat), F32),
            ),
            in_specs=[pl.BlockSpec(memory_space=pltpu.HBM)] * 11,
            out_specs=(vmem,) * 4,
            scratch_shapes=scratch,
            compiler_params=pltpu.CompilerParams(
                collective_id=0, has_side_effects=True, vmem_limit_bytes=63 << 20
            ),
        )(
            queries,
            owner.reshape(1, n),
            row.reshape(1, n),
            positive.reshape(1, n),
            table,
            w_in,
            w_out,
            tools,
            gain,
            bias_out,
            bias_in,
        )
        results = (updated, loss, qgrad, tgrad)
        hbm = pl.BlockSpec(memory_space=pltpu.HBM)
        updated, loss, qgrad, tgrad = pl.pallas_call(
            hand_over,
            out_shape=tuple(jax.ShapeDtypeStruct(r.shape, r.dtype) for r in results),
            in_specs=[hbm] * 4,
            out_specs=(hbm,) * 4,
            scratch_shapes=[pltpu.SemaphoreType.DMA((4,))],
            compiler_params=pltpu.CompilerParams(vmem_limit_bytes=63 << 20),
        )(*results)
        return updated, loss.reshape(n), qgrad, tgrad

    in_specs = (
        P(("dp", "mp"), None),
        P(("dp", "mp"), None),
        P(("dp", "mp")),
        P("mp", None),
        P(),
        P("mp", None),
        P("mp"),
        P("mp", None),
        P(),
        P("dp", None),
        P(("dp", "mp")),
    )
    out_specs = (P(("dp", "mp"), None), P(("dp", "mp")), P(("dp", "mp"), None), P("dp", None))
    return jax.shard_map(local, mesh=mesh, in_specs=in_specs, out_specs=out_specs, check_vma=False)
```

```python
import functools

import jax
import jax.numpy as jnp
from jax import lax
from jax.experimental import pallas as pl
from jax.experimental.pallas import tpu as pltpu
from jax.sharding import PartitionSpec as P

MESH = pl.DeviceIdType.MESH
BF, F32, I32 = jnp.bfloat16, jnp.float32, jnp.int32
NZ, NX, NYL, NYH, NC = 8, 4, 2, 4, 2
NP = NX * NYL
CAP = 4
N_SEMS = 192


def iota(shape, axis):
    return lax.broadcasted_iota(I32, shape, axis)


def bits(mask):
    return jnp.where(mask, 1.0, 0.0).astype(BF)


def dot(a, b):
    return jnp.dot(a, b, preferred_element_type=F32)


def dot_t(a, b):
    return lax.dot_general(a, b, (((1,), (1,)), ((), ())), preferred_element_type=F32)


def gelu(u):
    return 0.5 * u * (1.0 + jnp.tanh(0.7978845608028654 * (u + 0.044715 * (u * u * u))))


def kernel(
    grad_scale,
    queries_hbm,
    owner_hbm,
    row_hbm,
    positive_hbm,
    table_hbm,
    w_in,
    w_out,
    tools,
    gain_hbm,
    bias_out_hbm,
    bias_in_hbm,
    updated_ref,
    loss_ref,
    qgrad_ref,
    tgrad_ref,
    queries,
    owner_ref,
    row_ref,
    positive,
    table,
    gain_ref,
    bias_out_ref,
    bias_in_ref,
    bias_mat,
    wb,
    toolsb,
    req1,
    rcv1,
    req2,
    rcv2,
    g1b,
    ra,
    bb,
    fb,
    nbuf,
    pbuf,
    rbuf,
    updb,
    wgb,
    wga,
    s1b,
    s1r,
    s2b,
    s2r,
    s3b,
    s3r,
    s4r,
    send_sems,
    recv_sems,
    local_sems,
):
    d, m = lax.axis_index("dp"), lax.axis_index("mp")
    yh, c = lax.div(d, NC), lax.rem(d, NC)
    z, p = lax.div(m, NP), lax.rem(m, NP)
    x, yl = lax.div(p, NYL), lax.rem(p, NYL)
    chains, feat = queries.shape
    units = w_in.shape[0]
    split = 2 * units // 3

    def z_peer(o):
        return {"mp": lax.rem(z + o, NZ) * NP + p}

    def p_peer(o):
        return {"mp": z * NP + lax.rem(p + o, NP)}

    def x_peer(o):
        return {"mp": z * NP + lax.rem(x + o, NX) * NYL + yl}

    def y_peer(o):
        return {"dp": lax.rem(yh + o, NYH) * NC + c}

    other_core = {"dp": yh * NC + (1 - c)}
    y_flip = {"mp": z * NP + x * NYL + (1 - yl)}
    z_next = {"mp": lax.rem(z + 1 + (NZ - 2) * c, NZ) * NP + p}
    z_prev = {"mp": lax.rem(z + (NZ - 1) - (NZ - 2) * c, NZ) * NP + p}
    x_next = {"mp": z * NP + lax.rem(x + 1 + (NX - 2) * c, NX) * NYL + yl}
    x_prev = {"mp": z * NP + lax.rem(x + (NX - 1) - (NX - 2) * c, NX) * NYL + yl}

    def zb(k):
        return lax.rem(z - k + 2 * k * c + NZ, NZ)

    def xb(k):
        return lax.rem(x - k + 2 * k * c + NX, NX)

    count = [0]
    started = []
    arrived = set()

    def remote(src, dst, peer):
        i = count[0]
        count[0] += 1
        return pltpu.make_async_remote_copy(
            src_ref=src,
            dst_ref=dst,
            send_sem=send_sems.at[i],
            recv_sem=recv_sems.at[i],
            device_id=peer,
            device_id_type=MESH,
        )

    def send(src, dst, peer):
        copy = remote(src, dst, peer)
        copy.start()
        started.append(copy)
        return copy

    def arrive(copies):
        for copy in copies:
            if id(copy) not in arrived:
                arrived.add(id(copy))
                copy.wait_recv()

    barrier = pltpu.get_barrier_semaphore()
    peers = [z_peer(o) for o in range(1, NZ)] + [p_peer(o) for o in range(1, NP)]
    peers += [y_peer(o) for o in range(1, NYH)] + [other_core]
    for peer in peers:
        pl.semaphore_signal(barrier, inc=1, device_id=peer, device_id_type=MESH)

    def load(src, dst, i):
        copy = pltpu.make_async_copy(src, dst, local_sems.at[i])
        copy.start()
        return copy

    smalls = [
        (owner_hbm, owner_ref),
        (row_hbm, row_ref),
        (positive_hbm, positive),
        (gain_hbm, gain_ref),
        (bias_out_hbm, bias_out_ref),
        (bias_in_hbm, bias_in_ref),
    ]
    small_loads = [load(src, dst, 7 + i) for i, (src, dst) in enumerate(smalls)]
    table_load = load(table_hbm, table, 2)
    queries_load = load(queries_hbm, queries, 3)
    own_tools = load(tools, toolsb.at[c * NYH + yh], 4)
    for copy in small_loads:
        copy.wait()
    gain = gain_ref[...].astype(F32).reshape(1, feat)
    bias_out = bias_out_ref[...].astype(F32).reshape(1, feat)
    bias_in = jnp.pad(bias_in_ref[...].astype(F32).reshape(1, units), ((0, 0), (0, 128 - units)))

    eye = iota((chains, chains), 0) == iota((chains, chains), 1)
    owner_row = owner_ref[...]
    owner = jnp.sum(jnp.where(eye, owner_row.astype(F32), 0.0), axis=1, keepdims=True).astype(I32)
    own_mask = owner == iota((chains, NZ * NP), 1)
    earlier = bits(iota((chains, chains), 1) < iota((chains, chains), 0))
    prior = dot(earlier, bits(own_mask))
    rank = jnp.sum(jnp.where(own_mask, prior, 0.0), axis=1, keepdims=True).astype(I32)
    row_col = jnp.sum(jnp.where(eye, row_ref[...].astype(F32), 0.0), axis=1, keepdims=True)
    lane_of = (owner & (NP - 1)) * CAP + rank
    spread = jnp.where(iota((chains, 128), 1) == lane_of, row_col, 0.0).astype(BF)
    to_z = bits((owner_row >> 3) == iota((16, chains), 0))
    bias_line = jnp.where(iota((16, 128), 0) == NZ, bias_in, 0.0)
    req1[...] = dot(to_z, spread) + bias_line
    rcv1[z] = req1[...]
    pl.semaphore_wait(barrier, len(peers))
    reqs1 = [send(req1, rcv1.at[z], z_peer(o)) for o in range(1, NZ)]

    in_slot, out_slot = wb.at[z, x, 0:units], wb.at[z, x, units : 2 * units]
    y_in = remote(w_in, in_slot, y_flip)
    y_out = remote(w_out, out_slot, y_flip)
    own_in = pltpu.make_async_copy(w_in, in_slot, local_sems.at[5])
    own_out = pltpu.make_async_copy(w_out, out_slot, local_sems.at[6])

    @pl.when(c == yl)
    def _():
        y_in.start()
        y_out.start()
        own_in.start()
        own_out.start()

    @pl.when(c == yl)
    def _():
        own_in.wait()
        own_out.wait()

    @pl.when(c != yl)
    def _():
        y_in.wait_recv()
        y_out.wait_recv()

    def a_part(zz, xx):
        return wb.at[zz, xx, 0:split]

    def b_part(zz, xx):
        return wb.at[zz, xx, split : 2 * units]

    a_x = {NX - o: send(a_part(z, x), a_part(z, x), x_peer(o)) for o in range(1, NX)}
    a_next, a_prev, b_next, b_prev, b_x = {}, {}, {}, {}, {}

    def a_step(k, j):
        xj = lax.rem(x + j, NX)
        if k == 1 and j > 0:
            arrive([a_x[j]])
        if k > 1:
            arrive([a_next[k - 1, j]])
        src = a_part(zb(k - 1), xj)
        a_next[k, j] = send(src, src, z_next)
        if k <= 3:
            if k > 1:
                arrive([a_prev[k - 1, j]])
            src = a_part(zb(1 - k), xj)
            a_prev[k, j] = send(src, src, z_prev)

    def b_cross(k):
        if k:
            arrive([b_next[k] if k > 0 else b_prev[-k]])
        src = b_part(zb(k), x)
        b_x[k, 1] = send(src, src, x_next)
        b_x[k, -1] = send(src, src, x_prev)

    def b_relay(k):
        arrive([b_x[k, 1]])
        src = b_part(zb(k), xb(1))
        b_x[k, 2] = send(src, src, x_next)

    def b_step(k):
        if k > 1:
            arrive([b_next[k - 1]])
        src = b_part(zb(k - 1), x)
        b_next[k] = send(src, src, z_next)
        if k <= 3:
            if k > 1:
                arrive([b_prev[k - 1]])
            src = b_part(zb(1 - k), x)
            b_prev[k] = send(src, src, z_prev)

    b_step(1)
    a_step(1, 0)
    b_cross(0)

    arrive(reqs1)
    for zz in range(NZ):
        tile = rcv1[zz]
        mine = jnp.where(iota((16, 128), 0) == z, tile, 0.0)
        req2[zz : zz + 1, :] = jnp.sum(mine, axis=0, keepdims=True)
        req2[NZ + zz : NZ + zz + 1, :] = tile[NZ : NZ + 1, :]
    rcv2[p] = req2[...]
    reqs2 = [send(req2, rcv2.at[p], p_peer(o)) for o in range(1, NP)]

    b_step(2)
    b_cross(1)
    b_cross(-1)
    for j in range(1, NX):
        a_step(1, j)
    b_relay(0)

    arrive(reqs2)
    table_load.wait()
    asked = jnp.concatenate([rcv2[pp, 0:NZ, :] for pp in range(NP)], axis=0).astype(BF)
    slots = NZ * NP * CAP
    thrice = dot(bits((iota((slots, NZ * NP), 0) >> 2) == iota((slots, NZ * NP), 1)), asked)
    lane_mine = iota((slots, 128), 1) == (iota((slots, 128), 0) & (CAP - 1)) + CAP * p
    wanted = jnp.sum(jnp.where(lane_mine, thrice, 0.0), axis=1, keepdims=True).astype(I32)
    pick = bits(wanted == iota((slots, table.shape[0]), 1))
    g1b[...] = dot(pick, table[...]).astype(BF).reshape(g1b.shape)
    ra[p] = g1b[p]
    rows1 = [send(g1b.at[lax.rem(p + o, NP)], ra.at[p], p_peer(o)) for o in range(1, NP)]

    b_step(3)
    b_cross(2)
    b_cross(-2)
    a_step(2, 0)
    a_step(2, 1)
    b_relay(1)
    b_relay(-1)

    arrive(rows1)
    i0 = iota((slots, slots), 0)
    order1 = ((i0 >> 2) & (NP - 1)) * 32 + (i0 >> 5) * CAP + (i0 & (CAP - 1))
    regrouped = dot(bits(order1 == iota((slots, slots), 1)), ra[...].reshape(slots, -1))
    bb[...] = regrouped.astype(BF).reshape(bb.shape)
    fb[z] = bb[z]
    tool_sends = [send(tools, toolsb.at[c * NYH + yh], y_peer(o)) for o in range(1, NYH)]
    tool_swaps = [send(tools, toolsb.at[c * NYH + yh], other_core)]
    rows2 = [send(bb.at[lax.rem(z + o, NZ)], fb.at[z], z_peer(o)) for o in range(1, NZ)]

    b_step(4)
    b_cross(3)
    b_cross(-3)
    a_step(2, 2)
    a_step(2, 3)
    b_relay(2)
    b_relay(-2)
    b_cross(4)
    a_step(3, 0)
    a_step(3, 1)
    b_relay(3)
    b_relay(-3)

    width = NX * units
    bias_rows = jnp.concatenate([rcv2[NYL * xx + c, NZ : 2 * NZ, :] for xx in range(NX)], axis=1)
    line = iota((NX * 128, width), 0)
    lane_to = bits(((line & 127) < units) & (iota((NX * 128, width), 1) == (line >> 7) * units + (line & 127)))
    bias_mat[...] = dot(bias_rows.astype(BF), lane_to)
    queries_load.wait()

    arrive(rows2)
    select = bits(owner * CAP + rank == iota((chains, slots), 1))
    combined = queries[...].astype(F32) + dot(select, fb[...].reshape(slots, -1))
    centred = combined - jnp.mean(combined, axis=1, keepdims=True)
    spread_sq = jnp.mean(centred * centred, axis=1, keepdims=True)
    normed = centred * lax.rsqrt(spread_sq + 1e-05) * gain
    nbuf[c] = normed.astype(BF)
    swap_n = send(nbuf.at[c], nbuf.at[c], other_core)

    a_step(3, 2)
    a_step(3, 3)
    b_relay(4)

    arrive([swap_n])
    both = nbuf[...].reshape(2 * chains, feat)

    def hidden(k):
        if k:
            arrive([(a_next if k > 0 else a_prev)[abs(k), j] for j in range(NX)])
        arrive([b_x[k, -1], b_x[k, 2]])
        zz = zb(k)
        pre = dot_t(both, wb[zz, :, 0:units].reshape(width, feat)) + bias_mat[pl.ds(zz, 1), :]
        term = dot(gelu(pre).astype(BF), wb[zz, :, units : 2 * units].reshape(width, feat)).reshape(pbuf.shape)
        pbuf[...] = term if k == 0 else pbuf[...] + term

    hidden(0)
    for j in range(NX):
        a_step(4, j)
    arrive(tool_sends)
    for o in range(1, NYH):
        slot = toolsb.at[c * NYH + lax.rem(yh + o, NYH)]
        tool_swaps.append(send(slot, slot, other_core))
    for k in (1, -1, 2, -2, 3, -3, 4):
        hidden(k)
    swap_p = send(pbuf.at[1 - c], rbuf, other_core)
    arrive([swap_p])
    updated = (combined + (pbuf[c] + rbuf[...]) + bias_out).astype(BF)
    updated_ref[...] = updated
    updb[c] = updated
    swap_u = send(updb.at[c], updb.at[c], other_core)

    arrive(tool_swaps)
    own_tools.wait()
    all_tools = toolsb[...].reshape(NC * NYH * tools.shape[0], -1)
    n_tools = all_tools.shape[0]
    half = n_tools // 2
    scores = dot_t(updated, all_tools)
    pos = jnp.sum(jnp.where(eye, positive[...].astype(F32), 0.0), axis=1, keepdims=True).astype(I32)
    pos_col = ((pos >> 6) & 1) * half + (pos >> 7) * 64 + (pos & 63)
    is_pos = iota((chains, n_tools), 1) == pos_col
    top = jnp.max(scores, axis=1, keepdims=True)
    log_total = top + jnp.log(jnp.sum(jnp.exp(scores - top), axis=1, keepdims=True))
    loss = log_total - jnp.sum(jnp.where(is_pos, scores, 0.0), axis=1, keepdims=True)
    grad = (jnp.exp(scores - log_total) - jnp.where(is_pos, 1.0, 0.0)).astype(BF)
    wgb[0] = grad[:, :half]
    wgb[1] = grad[:, half:]
    swap_w = send(wgb.at[1 - c], wga.at[c], other_core)
    wga[c] = wgb[c]

    arrive([swap_u, swap_w])
    i1 = iota((half, half), 0)
    order2 = ((i1 >> 3) & (NYH - 1)) * 64 + (i1 >> 5) * 8 + (i1 & 7)
    grad_t = dot_t(bits(order2 == iota((half, half), 1)), wga[...].reshape(2 * chains, half)).astype(BF)
    part = dot(grad_t, updb[...].reshape(2 * chains, -1))
    s1b[...] = part.astype(BF).reshape(s1b.shape)
    s1r[p] = s1b[p]
    stage1 = [send(s1b.at[lax.rem(p + o, NP)], s1r.at[p], p_peer(o)) for o in range(1, NP)]
    loss_ref[...] = jnp.sum(jnp.where(eye, loss, 0.0), axis=0, keepdims=True)
    qgrad_ref[...] = dot(grad, all_tools)
    arrive(stage1)
    total = s1r[0].astype(F32)
    for i in range(1, NP):
        total = total + s1r[i].astype(F32)
    s2b[...] = total.reshape(s2b.shape).astype(BF)
    s2r[yh] = s2b[yh]
    arrive([send(s2b.at[lax.rem(yh + o, NYH)], s2r.at[yh], y_peer(o)) for o in range(1, NYH)])
    total = s2r[0].astype(F32)
    for i in range(1, NYH):
        total = total + s2r[i].astype(F32)
    s3b[...] = total.astype(BF)
    s3r[z] = s3b[...]
    arrive([send(s3b, s3r.at[z], z_peer(o)) for o in range(1, NZ)])
    total = s3r[0].astype(F32)
    for i in range(1, NZ):
        total = total + s3r[i].astype(F32)
    s4r[p] = (total * grad_scale).astype(BF)
    arrive([send(s4r.at[p], s4r.at[p], p_peer(o)) for o in range(1, NP)])
    tgrad_ref[...] = s4r[...].astype(F32).reshape(tgrad_ref.shape)

    for copy in started:
        copy.wait_send()

    @pl.when(c == yl)
    def _():
        y_in.wait_send()
        y_out.wait_send()


def hand_over(*refs):
    held, sems = refs[8:12], refs[12]
    copies_in = [pltpu.make_async_copy(refs[i], held[i], sems.at[i]) for i in range(4)]
    copies_out = [pltpu.make_async_copy(held[i], refs[4 + i], sems.at[4 + i]) for i in range(4)]
    for copy in copies_in:
        copy.start()
    for copy_in, copy_out in zip(copies_in, copies_out):
        copy_in.wait()
        copy_out.start()
    for copy in copies_out:
        copy.wait()


def solution(mesh):
    def local(queries, owner, row, table, gain, w_in, bias_in, w_out, bias_out, tools, positive):
        n, feat = queries.shape
        units = w_in.shape[0]
        block = tools.shape[0]
        scale = (block * mesh.shape["dp"] / (n * mesh.shape["dp"] * mesh.shape["mp"])) ** 0.5
        vmem = pl.BlockSpec(memory_space=pltpu.VMEM)
        slot_rows = NP * CAP
        sub = block // NP
        scratch = [
            pltpu.VMEM((n, feat), BF),
            pltpu.VMEM((1, n), I32),
            pltpu.VMEM((1, n), I32),
            pltpu.VMEM((1, n), I32),
            pltpu.VMEM(table.shape, BF),
            pltpu.VMEM((feat,), BF),
            pltpu.VMEM((feat,), BF),
            pltpu.VMEM((units,), BF),
            pltpu.VMEM((NZ, NX * units), F32),
            pltpu.VMEM((NZ, NX, 2 * units, feat), BF),
            pltpu.VMEM((NC * NYH, block, feat), BF),
            pltpu.VMEM((16, 128), F32),
            pltpu.VMEM((NZ, 16, 128), F32),
            pltpu.VMEM((16, 128), F32),
            pltpu.VMEM((NP, 16, 128), F32),
            pltpu.VMEM((NP, slot_rows, feat), BF),
            pltpu.VMEM((NP, slot_rows, feat), BF),
            pltpu.VMEM((NZ, slot_rows, feat), BF),
            pltpu.VMEM((NZ, slot_rows, feat), BF),
            pltpu.VMEM((NC, n, feat), BF),
            pltpu.VMEM((NC, n, feat), F32),
            pltpu.VMEM((n, feat), F32),
            pltpu.VMEM((NC, n, feat), BF),
            pltpu.VMEM((NC, n, NYH * block), BF),
            pltpu.VMEM((NC, n, NYH * block), BF),
            pltpu.VMEM((NP, NYH * sub, feat), BF),
            pltpu.VMEM((NP, NYH * sub, feat), BF),
            pltpu.VMEM((NYH, sub, feat), BF),
            pltpu.VMEM((NYH, sub, feat), BF),
            pltpu.VMEM((sub, feat), BF),
            pltpu.VMEM((NZ, sub, feat), BF),
            pltpu.VMEM((NP, sub, feat), BF),
            pltpu.SemaphoreType.DMA((N_SEMS,)),
            pltpu.SemaphoreType.DMA((N_SEMS,)),
            pltpu.SemaphoreType.DMA((13,)),
        ]
        updated, loss, qgrad, tgrad = pl.pallas_call(
            functools.partial(kernel, scale),
            out_shape=(
                jax.ShapeDtypeStruct((n, feat), BF),
                jax.ShapeDtypeStruct((1, n), F32),
                jax.ShapeDtypeStruct((n, feat), F32),
                jax.ShapeDtypeStruct((block, feat), F32),
            ),
            in_specs=[pl.BlockSpec(memory_space=pltpu.HBM)] * 11,
            out_specs=(vmem,) * 4,
            scratch_shapes=scratch,
            compiler_params=pltpu.CompilerParams(
                collective_id=0, has_side_effects=True, vmem_limit_bytes=63 << 20
            ),
        )(
            queries,
            owner.reshape(1, n),
            row.reshape(1, n),
            positive.reshape(1, n),
            table,
            w_in,
            w_out,
            tools,
            gain,
            bias_out,
            bias_in,
        )
        results = (updated, loss, qgrad, tgrad)
        hbm = pl.BlockSpec(memory_space=pltpu.HBM)
        updated, loss, qgrad, tgrad = pl.pallas_call(
            hand_over,
            out_shape=tuple(jax.ShapeDtypeStruct(r.shape, r.dtype) for r in results),
            in_specs=[hbm] * 4,
            out_specs=(hbm,) * 4,
            scratch_shapes=[pltpu.VMEM(r.shape, r.dtype) for r in results] + [pltpu.SemaphoreType.DMA((8,))],
            compiler_params=pltpu.CompilerParams(vmem_limit_bytes=63 << 20),
        )(*results)
        return updated, loss.reshape(n), qgrad, tgrad

    in_specs = (
        P(("dp", "mp"), None),
        P(("dp", "mp"), None),
        P(("dp", "mp")),
        P("mp", None),
        P(),
        P("mp", None),
        P("mp"),
        P("mp", None),
        P(),
        P("dp", None),
        P(("dp", "mp")),
    )
    out_specs = (P(("dp", "mp"), None), P(("dp", "mp")), P(("dp", "mp"), None), P("dp", None))
    return jax.shard_map(local, mesh=mesh, in_specs=in_specs, out_specs=out_specs, check_vma=False)
```

```python
import functools

import jax
import jax.numpy as jnp
from jax import lax
from jax.experimental import pallas as pl
from jax.experimental.pallas import tpu as pltpu
from jax.sharding import PartitionSpec as P

MESH = pl.DeviceIdType.MESH
BF, F32, I32 = jnp.bfloat16, jnp.float32, jnp.int32
NZ, NX, NYL, NYH, NC = 8, 4, 2, 4, 2
NP = NX * NYL
CAP = 4
N_SEMS = 192


def iota(shape, axis):
    return lax.broadcasted_iota(I32, shape, axis)


def bits(mask):
    return jnp.where(mask, 1.0, 0.0).astype(BF)


def dot(a, b):
    return jnp.dot(a, b, preferred_element_type=F32)


def dot_t(a, b):
    return lax.dot_general(a, b, (((1,), (1,)), ((), ())), preferred_element_type=F32)


def gelu(u):
    return 0.5 * u * (1.0 + jnp.tanh(0.7978845608028654 * (u + 0.044715 * (u * u * u))))


def kernel(
    grad_scale,
    queries_hbm,
    owner_hbm,
    row_hbm,
    positive_hbm,
    table_hbm,
    w_in,
    w_out,
    tools,
    gain_hbm,
    bias_out_hbm,
    bias_in_hbm,
    updated_hbm,
    loss_ref,
    qgrad_hbm,
    tgrad_ref,
    queries,
    owner_ref,
    row_ref,
    positive,
    table,
    gain_ref,
    bias_out_ref,
    bias_in_ref,
    bias_mat,
    wb,
    toolsb,
    req1,
    rcv1,
    req2,
    rcv2,
    g1b,
    ra,
    bb,
    fb,
    nbuf,
    pbuf,
    rbuf,
    updb,
    wgb,
    wga,
    s1b,
    s1r,
    s2b,
    s2r,
    s3r,
    s4r,
    qgrad_buf,
    send_sems,
    recv_sems,
    local_sems,
):
    d, m = lax.axis_index("dp"), lax.axis_index("mp")
    yh, c = lax.div(d, NC), lax.rem(d, NC)
    z, p = lax.div(m, NP), lax.rem(m, NP)
    x, yl = lax.div(p, NYL), lax.rem(p, NYL)
    chains, feat = queries.shape
    units = w_in.shape[0]
    split = 2 * units // 3

    def z_peer(o):
        return {"mp": lax.rem(z + o, NZ) * NP + p}

    def p_peer(o):
        return {"mp": z * NP + lax.rem(p + o, NP)}

    def x_peer(o):
        return {"mp": z * NP + lax.rem(x + o, NX) * NYL + yl}

    def y_peer(o):
        return {"dp": lax.rem(yh + o, NYH) * NC + c}

    other_core = {"dp": yh * NC + (1 - c)}
    y_flip = {"mp": z * NP + x * NYL + (1 - yl)}
    z_next = {"mp": lax.rem(z + 1 + (NZ - 2) * c, NZ) * NP + p}
    z_prev = {"mp": lax.rem(z + (NZ - 1) - (NZ - 2) * c, NZ) * NP + p}
    x_next = {"mp": z * NP + lax.rem(x + 1 + (NX - 2) * c, NX) * NYL + yl}
    x_prev = {"mp": z * NP + lax.rem(x + (NX - 1) - (NX - 2) * c, NX) * NYL + yl}

    def zb(k):
        return lax.rem(z - k + 2 * k * c + NZ, NZ)

    def xb(k):
        return lax.rem(x - k + 2 * k * c + NX, NX)

    count = [0]
    started = []
    arrived = set()

    def remote(src, dst, peer):
        i = count[0]
        count[0] += 1
        return pltpu.make_async_remote_copy(
            src_ref=src,
            dst_ref=dst,
            send_sem=send_sems.at[i],
            recv_sem=recv_sems.at[i],
            device_id=peer,
            device_id_type=MESH,
        )

    def send(src, dst, peer):
        copy = remote(src, dst, peer)
        copy.start()
        started.append(copy)
        return copy

    def arrive(copies):
        for copy in copies:
            if id(copy) not in arrived:
                arrived.add(id(copy))
                copy.wait_recv()

    halves = range(2)
    half_feat = feat // 2
    cuts = [slice(h * half_feat, (h + 1) * half_feat) for h in halves]

    def spread_out(buf, got, me, count, peer_of):
        got[me] = buf[me]
        return [send(buf.at[lax.rem(me + o, count)], got.at[me], peer_of(o)) for o in range(1, count)]

    def added(got, count):
        total = got[0].astype(F32)
        for i in range(1, count):
            total = total + got[i].astype(F32)
        return total

    barrier = pltpu.get_barrier_semaphore()
    peers = [z_peer(o) for o in range(1, NZ)] + [p_peer(o) for o in range(1, NP)]
    peers += [y_peer(o) for o in range(1, NYH)] + [other_core]
    for peer in peers:
        pl.semaphore_signal(barrier, inc=1, device_id=peer, device_id_type=MESH)

    def load(src, dst, i):
        copy = pltpu.make_async_copy(src, dst, local_sems.at[i])
        copy.start()
        return copy

    smalls = [
        (owner_hbm, owner_ref),
        (row_hbm, row_ref),
        (positive_hbm, positive),
        (gain_hbm, gain_ref),
        (bias_out_hbm, bias_out_ref),
        (bias_in_hbm, bias_in_ref),
    ]
    small_loads = [load(src, dst, 7 + i) for i, (src, dst) in enumerate(smalls)]
    table_load = load(table_hbm, table, 2)
    queries_load = load(queries_hbm, queries, 3)
    own_tools = load(tools, toolsb.at[c * NYH + yh], 4)
    for copy in small_loads:
        copy.wait()
    gain = gain_ref[...].astype(F32).reshape(1, feat)
    bias_out = bias_out_ref[...].astype(F32).reshape(1, feat)
    bias_in = jnp.pad(bias_in_ref[...].astype(F32).reshape(1, units), ((0, 0), (0, 128 - units)))

    eye = iota((chains, chains), 0) == iota((chains, chains), 1)
    owner_row = owner_ref[...]
    owner = jnp.sum(jnp.where(eye, owner_row.astype(F32), 0.0), axis=1, keepdims=True).astype(I32)
    own_mask = owner == iota((chains, NZ * NP), 1)
    earlier = bits(iota((chains, chains), 1) < iota((chains, chains), 0))
    prior = dot(earlier, bits(own_mask))
    rank = jnp.sum(jnp.where(own_mask, prior, 0.0), axis=1, keepdims=True).astype(I32)
    row_col = jnp.sum(jnp.where(eye, row_ref[...].astype(F32), 0.0), axis=1, keepdims=True)
    lane_of = (owner & (NP - 1)) * CAP + rank
    spread = jnp.where(iota((chains, 128), 1) == lane_of, row_col, 0.0).astype(BF)
    to_z = bits((owner_row >> 3) == iota((16, chains), 0))
    bias_line = jnp.where(iota((16, 128), 0) == NZ, bias_in, 0.0)
    req1[...] = dot(to_z, spread) + bias_line
    rcv1[z] = req1[...]
    pl.semaphore_wait(barrier, len(peers))
    reqs1 = [send(req1, rcv1.at[z], z_peer(o)) for o in range(1, NZ)]

    in_slot, out_slot = wb.at[z, x, 0:units], wb.at[z, x, units : 2 * units]
    y_in = remote(w_in, in_slot, y_flip)
    y_out = remote(w_out, out_slot, y_flip)
    own_in = pltpu.make_async_copy(w_in, in_slot, local_sems.at[5])
    own_out = pltpu.make_async_copy(w_out, out_slot, local_sems.at[6])

    @pl.when(c == yl)
    def _():
        y_in.start()
        y_out.start()
        own_in.start()
        own_out.start()

    @pl.when(c == yl)
    def _():
        own_in.wait()
        own_out.wait()

    @pl.when(c != yl)
    def _():
        y_in.wait_recv()
        y_out.wait_recv()

    def a_part(zz, xx):
        return wb.at[zz, xx, 0:split]

    def b_part(zz, xx):
        return wb.at[zz, xx, split : 2 * units]

    a_x = {NX - o: send(a_part(z, x), a_part(z, x), x_peer(o)) for o in range(1, NX)}
    a_next, a_prev, b_next, b_prev, b_x = {}, {}, {}, {}, {}

    def a_step(k, j):
        xj = lax.rem(x + j, NX)
        if k == 1 and j > 0:
            arrive([a_x[j]])
        if k > 1:
            arrive([a_next[k - 1, j]])
        src = a_part(zb(k - 1), xj)
        a_next[k, j] = send(src, src, z_next)
        if k <= 3:
            if k > 1:
                arrive([a_prev[k - 1, j]])
            src = a_part(zb(1 - k), xj)
            a_prev[k, j] = send(src, src, z_prev)

    def b_cross(k):
        if k:
            arrive([b_next[k] if k > 0 else b_prev[-k]])
        src = b_part(zb(k), x)
        b_x[k, 1] = send(src, src, x_next)
        b_x[k, -1] = send(src, src, x_prev)

    def b_relay(k):
        arrive([b_x[k, 1]])
        src = b_part(zb(k), xb(1))
        b_x[k, 2] = send(src, src, x_next)

    def b_step(k):
        if k > 1:
            arrive([b_next[k - 1]])
        src = b_part(zb(k - 1), x)
        b_next[k] = send(src, src, z_next)
        if k <= 3:
            if k > 1:
                arrive([b_prev[k - 1]])
            src = b_part(zb(1 - k), x)
            b_prev[k] = send(src, src, z_prev)

    b_step(1)
    a_step(1, 0)
    b_cross(0)

    arrive(reqs1)
    for zz in range(NZ):
        tile = rcv1[zz]
        mine = jnp.where(iota((16, 128), 0) == z, tile, 0.0)
        req2[zz : zz + 1, :] = jnp.sum(mine, axis=0, keepdims=True)
        req2[NZ + zz : NZ + zz + 1, :] = tile[NZ : NZ + 1, :]
    rcv2[p] = req2[...]
    reqs2 = [send(req2, rcv2.at[p], p_peer(o)) for o in range(1, NP)]

    b_step(2)
    b_cross(1)
    b_cross(-1)
    for j in range(1, NX):
        a_step(1, j)
    b_relay(0)

    arrive(reqs2)
    table_load.wait()
    asked = jnp.concatenate([rcv2[pp, 0:NZ, :] for pp in range(NP)], axis=0).astype(BF)
    slots = NZ * NP * CAP
    thrice = dot(bits((iota((slots, NZ * NP), 0) >> 2) == iota((slots, NZ * NP), 1)), asked)
    lane_mine = iota((slots, 128), 1) == (iota((slots, 128), 0) & (CAP - 1)) + CAP * p
    wanted = jnp.sum(jnp.where(lane_mine, thrice, 0.0), axis=1, keepdims=True).astype(I32)
    pick = bits(wanted == iota((slots, table.shape[0]), 1))
    rows1, rows2 = [], []
    for h in halves:
        g1b[h] = dot(pick, table[:, cuts[h]]).astype(BF).reshape(g1b.shape[1:])
        rows1.append(spread_out(g1b.at[h], ra.at[h], p, NP, p_peer))

    b_step(3)
    b_cross(2)
    b_cross(-2)
    a_step(2, 0)
    a_step(2, 1)
    b_relay(1)
    b_relay(-1)

    i0 = iota((slots, slots), 0)
    order1 = ((i0 >> 2) & (NP - 1)) * 32 + (i0 >> 5) * CAP + (i0 & (CAP - 1))
    regroup = bits(order1 == iota((slots, slots), 1))
    for h in halves:
        arrive(rows1[h])
        bb[h] = dot(regroup, ra[h].reshape(slots, half_feat)).astype(BF).reshape(bb.shape[1:])
        rows2.append(spread_out(bb.at[h], fb.at[h], z, NZ, z_peer))
    tool_sends = [send(tools, toolsb.at[c * NYH + yh], y_peer(o)) for o in range(1, NYH)]
    tool_swaps = [send(tools, toolsb.at[c * NYH + yh], other_core)]

    b_step(4)
    b_cross(3)
    b_cross(-3)
    a_step(2, 2)
    a_step(2, 3)
    b_relay(2)
    b_relay(-2)
    b_cross(4)
    a_step(3, 0)
    a_step(3, 1)
    b_relay(3)
    b_relay(-3)

    width = NX * units
    bias_rows = jnp.concatenate([rcv2[NYL * xx + c, NZ : 2 * NZ, :] for xx in range(NX)], axis=1)
    line = iota((NX * 128, width), 0)
    lane_to = bits(((line & 127) < units) & (iota((NX * 128, width), 1) == (line >> 7) * units + (line & 127)))
    bias_mat[...] = dot(bias_rows.astype(BF), lane_to)
    queries_load.wait()

    arrive(rows2[0] + rows2[1])
    select = bits(owner * CAP + rank == iota((chains, slots), 1))
    first_rows = [dot(select, fb[h].reshape(slots, half_feat)) for h in halves]
    combined = queries[...].astype(F32) + jnp.concatenate(first_rows, axis=1)
    centred = combined - jnp.mean(combined, axis=1, keepdims=True)
    spread_sq = jnp.mean(centred * centred, axis=1, keepdims=True)
    normed = centred * lax.rsqrt(spread_sq + 1e-05) * gain
    nbuf[c] = normed.astype(BF)
    swap_n = send(nbuf.at[c], nbuf.at[c], other_core)

    a_step(3, 2)
    a_step(3, 3)
    b_relay(4)

    arrive([swap_n])
    both = nbuf[...].reshape(2 * chains, feat)

    def hidden(k):
        if k:
            arrive([(a_next if k > 0 else a_prev)[abs(k), j] for j in range(NX)])
        arrive([b_x[k, -1], b_x[k, 2]])
        zz = zb(k)
        pre = dot_t(both, wb[zz, :, 0:units].reshape(width, feat)) + bias_mat[pl.ds(zz, 1), :]
        term = dot(gelu(pre).astype(BF), wb[zz, :, units : 2 * units].reshape(width, feat)).reshape(pbuf.shape)
        pbuf[...] = term if k == 0 else pbuf[...] + term

    hidden(0)
    for j in range(NX):
        a_step(4, j)
    arrive(tool_sends)
    for o in range(1, NYH):
        slot = toolsb.at[c * NYH + lax.rem(yh + o, NYH)]
        tool_swaps.append(send(slot, slot, other_core))
    for k in (1, -1, 2, -2, 3, -3, 4):
        hidden(k)
    swap_p = send(pbuf.at[1 - c], rbuf, other_core)
    arrive([swap_p])
    updated = (combined + (pbuf[c] + rbuf[...]) + bias_out).astype(BF)
    updb[c] = updated
    swap_u = send(updb.at[c], updb.at[c], other_core)
    updated_out = load(updb.at[c], updated_hbm, 13)

    arrive(tool_swaps)
    own_tools.wait()
    all_tools = toolsb[...].reshape(NC * NYH * tools.shape[0], -1)
    n_tools = all_tools.shape[0]
    half = n_tools // 2
    scores = dot_t(updated, all_tools)
    pos = jnp.sum(jnp.where(eye, positive[...].astype(F32), 0.0), axis=1, keepdims=True).astype(I32)
    pos_col = ((pos >> 6) & 1) * half + (pos >> 7) * 64 + (pos & 63)
    is_pos = iota((chains, n_tools), 1) == pos_col
    top = jnp.max(scores, axis=1, keepdims=True)
    log_total = top + jnp.log(jnp.sum(jnp.exp(scores - top), axis=1, keepdims=True))
    loss = log_total - jnp.sum(jnp.where(is_pos, scores, 0.0), axis=1, keepdims=True)
    grad = (jnp.exp(scores - log_total) - jnp.where(is_pos, 1.0, 0.0)).astype(BF)
    wgb[0] = grad[:, :half]
    wgb[1] = grad[:, half:]
    swap_w = send(wgb.at[1 - c], wga.at[c], other_core)
    wga[c] = wgb[c]

    arrive([swap_u, swap_w])
    i1 = iota((half, half), 0)
    order2 = ((i1 >> 3) & (NYH - 1)) * 64 + (i1 >> 5) * 8 + (i1 & 7)
    grad_t = dot_t(bits(order2 == iota((half, half), 1)), wga[...].reshape(2 * chains, half)).astype(BF)
    stage1, stage2, stage3, stage4 = [], [], [], []
    for h in halves:
        part = dot(grad_t, updb[:, :, cuts[h]].reshape(2 * chains, half_feat))
        s1b[h] = part.astype(BF).reshape(s1b.shape[1:])
        stage1.append(spread_out(s1b.at[h], s1r.at[h], p, NP, p_peer))
    loss_ref[...] = jnp.sum(jnp.where(eye, loss, 0.0), axis=0, keepdims=True)
    qgrad_buf[...] = dot(grad, all_tools)
    qgrad_out = load(qgrad_buf, qgrad_hbm, 14)
    for h in halves:
        arrive(stage1[h])
        s2b[h] = added(s1r.at[h], NP).astype(BF).reshape(s2b.shape[1:])
        stage2.append(spread_out(s2b.at[h], s2r.at[h], yh, NYH, y_peer))
    for h in halves:
        arrive(stage2[h])
        s3r[h, z] = added(s2r.at[h], NYH).astype(BF)
        stage3.append([send(s3r.at[h, z], s3r.at[h, z], z_peer(o)) for o in range(1, NZ)])
    for h in halves:
        arrive(stage3[h])
        s4r[h, p] = (added(s3r.at[h], NZ) * grad_scale).astype(BF)
        stage4.append([send(s4r.at[h, p], s4r.at[h, p], p_peer(o)) for o in range(1, NP)])
    for h in halves:
        arrive(stage4[h])
        tgrad_ref[:, cuts[h]] = s4r[h].astype(F32).reshape(-1, half_feat)
    updated_out.wait()
    qgrad_out.wait()

    for copy in started:
        copy.wait_send()

    @pl.when(c == yl)
    def _():
        y_in.wait_send()
        y_out.wait_send()


def hand_over(*refs):
    held, sems = refs[8:12], refs[12]
    copies_in = [pltpu.make_async_copy(refs[i], held[i], sems.at[i]) for i in range(4)]
    copies_out = [pltpu.make_async_copy(held[i], refs[4 + i], sems.at[4 + i]) for i in range(4)]
    for copy in copies_in:
        copy.start()
    for copy_in, copy_out in zip(copies_in, copies_out):
        copy_in.wait()
        copy_out.start()
    for copy in copies_out:
        copy.wait()


def solution(mesh):
    def local(queries, owner, row, table, gain, w_in, bias_in, w_out, bias_out, tools, positive):
        n, feat = queries.shape
        units = w_in.shape[0]
        block = tools.shape[0]
        scale = (block * mesh.shape["dp"] / (n * mesh.shape["dp"] * mesh.shape["mp"])) ** 0.5
        vmem = pl.BlockSpec(memory_space=pltpu.VMEM)
        hbm = pl.BlockSpec(memory_space=pltpu.HBM)
        slot_rows = NP * CAP
        sub = block // NP
        scratch = [
            pltpu.VMEM((n, feat), BF),
            pltpu.VMEM((1, n), I32),
            pltpu.VMEM((1, n), I32),
            pltpu.VMEM((1, n), I32),
            pltpu.VMEM(table.shape, BF),
            pltpu.VMEM((feat,), BF),
            pltpu.VMEM((feat,), BF),
            pltpu.VMEM((units,), BF),
            pltpu.VMEM((NZ, NX * units), F32),
            pltpu.VMEM((NZ, NX, 2 * units, feat), BF),
            pltpu.VMEM((NC * NYH, block, feat), BF),
            pltpu.VMEM((16, 128), F32),
            pltpu.VMEM((NZ, 16, 128), F32),
            pltpu.VMEM((16, 128), F32),
            pltpu.VMEM((NP, 16, 128), F32),
            pltpu.VMEM((2, NP, slot_rows, feat // 2), BF),
            pltpu.VMEM((2, NP, slot_rows, feat // 2), BF),
            pltpu.VMEM((2, NZ, slot_rows, feat // 2), BF),
            pltpu.VMEM((2, NZ, slot_rows, feat // 2), BF),
            pltpu.VMEM((NC, n, feat), BF),
            pltpu.VMEM((NC, n, feat), F32),
            pltpu.VMEM((n, feat), F32),
            pltpu.VMEM((NC, n, feat), BF),
            pltpu.VMEM((NC, n, NYH * block), BF),
            pltpu.VMEM((NC, n, NYH * block), BF),
            pltpu.VMEM((2, NP, NYH * sub, feat // 2), BF),
            pltpu.VMEM((2, NP, NYH * sub, feat // 2), BF),
            pltpu.VMEM((2, NYH, sub, feat // 2), BF),
            pltpu.VMEM((2, NYH, sub, feat // 2), BF),
            pltpu.VMEM((2, NZ, sub, feat // 2), BF),
            pltpu.VMEM((2, NP, sub, feat // 2), BF),
            pltpu.VMEM((n, feat), F32),
            pltpu.SemaphoreType.DMA((N_SEMS,)),
            pltpu.SemaphoreType.DMA((N_SEMS,)),
            pltpu.SemaphoreType.DMA((15,)),
        ]
        updated, loss, qgrad, tgrad = pl.pallas_call(
            functools.partial(kernel, scale),
            out_shape=(
                jax.ShapeDtypeStruct((n, feat), BF),
                jax.ShapeDtypeStruct((1, n), F32),
                jax.ShapeDtypeStruct((n, feat), F32),
                jax.ShapeDtypeStruct((block, feat), F32),
            ),
            in_specs=[pl.BlockSpec(memory_space=pltpu.HBM)] * 11,
            out_specs=(hbm, vmem, hbm, vmem),
            scratch_shapes=scratch,
            compiler_params=pltpu.CompilerParams(
                collective_id=0, has_side_effects=True, vmem_limit_bytes=63 << 20
            ),
        )(
            queries,
            owner.reshape(1, n),
            row.reshape(1, n),
            positive.reshape(1, n),
            table,
            w_in,
            w_out,
            tools,
            gain,
            bias_out,
            bias_in,
        )
        results = (updated, loss, qgrad, tgrad)
        updated, loss, qgrad, tgrad = pl.pallas_call(
            hand_over,
            out_shape=tuple(jax.ShapeDtypeStruct(r.shape, r.dtype) for r in results),
            in_specs=[hbm] * 4,
            out_specs=(hbm,) * 4,
            scratch_shapes=[pltpu.VMEM(r.shape, r.dtype) for r in results] + [pltpu.SemaphoreType.DMA((8,))],
            compiler_params=pltpu.CompilerParams(vmem_limit_bytes=63 << 20),
        )(*results)
        return updated, loss.reshape(n), qgrad, tgrad

    in_specs = (
        P(("dp", "mp"), None),
        P(("dp", "mp"), None),
        P(("dp", "mp")),
        P("mp", None),
        P(),
        P("mp", None),
        P("mp"),
        P("mp", None),
        P(),
        P("dp", None),
        P(("dp", "mp")),
    )
    out_specs = (P(("dp", "mp"), None), P(("dp", "mp")), P(("dp", "mp"), None), P("dp", None))
    return jax.shard_map(local, mesh=mesh, in_specs=in_specs, out_specs=out_specs, check_vma=False)
```

```python
import functools

import jax
import jax.numpy as jnp
from jax import lax
from jax.experimental import pallas as pl
from jax.experimental.pallas import tpu as pltpu
from jax.sharding import PartitionSpec as P

MESH = pl.DeviceIdType.MESH
BF, F32, I32 = jnp.bfloat16, jnp.float32, jnp.int32
NZ, NX, NYL, NYH, NC = 8, 4, 2, 4, 2
NP = NX * NYL
CAP = 4
N_SEMS = 192


def iota(shape, axis):
    return lax.broadcasted_iota(I32, shape, axis)


def bits(mask):
    return jnp.where(mask, 1.0, 0.0).astype(BF)


def dot(a, b):
    return jnp.dot(a, b, preferred_element_type=F32)


def dot_t(a, b):
    return lax.dot_general(a, b, (((1,), (1,)), ((), ())), preferred_element_type=F32)


def gelu(u):
    return 0.5 * u * (1.0 + jnp.tanh(0.7978845608028654 * (u + 0.044715 * (u * u * u))))


def kernel(
    grad_scale,
    queries_hbm,
    owner_hbm,
    row_hbm,
    positive_hbm,
    table_hbm,
    w_in,
    w_out,
    tools,
    gain_hbm,
    bias_out_hbm,
    bias_in_hbm,
    updated_hbm,
    loss_ref,
    qgrad_hbm,
    tgrad_ref,
    queries,
    owner_ref,
    row_ref,
    positive,
    table,
    gain_ref,
    bias_out_ref,
    bias_in_ref,
    bias_mat,
    wb,
    toolsb,
    req1,
    rcv1,
    req2,
    rcv2,
    g1b,
    ra,
    bb,
    fb,
    nbuf,
    pbuf,
    rbuf,
    updb,
    wgb,
    wga,
    s1b,
    s1r,
    s2b,
    s2r,
    s3r,
    s4r,
    qgrad_buf,
    send_sems,
    recv_sems,
    local_sems,
):
    d, m = lax.axis_index("dp"), lax.axis_index("mp")
    yh, c = lax.div(d, NC), lax.rem(d, NC)
    z, p = lax.div(m, NP), lax.rem(m, NP)
    x, yl = lax.div(p, NYL), lax.rem(p, NYL)
    chains, feat = queries.shape
    units = w_in.shape[0]
    split = 2 * units // 3

    def z_peer(o):
        return {"mp": lax.rem(z + o, NZ) * NP + p}

    def p_peer(o):
        return {"mp": z * NP + lax.rem(p + o, NP)}

    def x_peer(o):
        return {"mp": z * NP + lax.rem(x + o, NX) * NYL + yl}

    def y_peer(o):
        return {"dp": lax.rem(yh + o, NYH) * NC + c}

    other_core = {"dp": yh * NC + (1 - c)}
    y_flip = {"mp": z * NP + x * NYL + (1 - yl)}
    z_next = {"mp": lax.rem(z + 1 + (NZ - 2) * c, NZ) * NP + p}
    z_prev = {"mp": lax.rem(z + (NZ - 1) - (NZ - 2) * c, NZ) * NP + p}
    x_next = {"mp": z * NP + lax.rem(x + 1 + (NX - 2) * c, NX) * NYL + yl}
    x_prev = {"mp": z * NP + lax.rem(x + (NX - 1) - (NX - 2) * c, NX) * NYL + yl}

    def zb(k):
        return lax.rem(z - k + 2 * k * c + NZ, NZ)

    def xb(k):
        return lax.rem(x - k + 2 * k * c + NX, NX)

    count = [0]
    started = []
    arrived = set()

    def remote(src, dst, peer):
        i = count[0]
        count[0] += 1
        return pltpu.make_async_remote_copy(
            src_ref=src,
            dst_ref=dst,
            send_sem=send_sems.at[i],
            recv_sem=recv_sems.at[i],
            device_id=peer,
            device_id_type=MESH,
        )

    def send(src, dst, peer):
        copy = remote(src, dst, peer)
        copy.start()
        started.append(copy)
        return copy

    def arrive(copies):
        for copy in copies:
            if id(copy) not in arrived:
                arrived.add(id(copy))
                copy.wait_recv()

    halves = range(2)
    half_feat = feat // 2
    cuts = [slice(h * half_feat, (h + 1) * half_feat) for h in halves]

    def spread_out(buf, got, me, count, peer_of):
        got[me] = buf[me]
        return [send(buf.at[lax.rem(me + o, count)], got.at[me], peer_of(o)) for o in range(1, count)]

    def added(got, count):
        total = got[0].astype(F32)
        for i in range(1, count):
            total = total + got[i].astype(F32)
        return total

    barrier = pltpu.get_barrier_semaphore()
    peers = [z_peer(o) for o in range(1, NZ)] + [p_peer(o) for o in range(1, NP)]
    peers += [y_peer(o) for o in range(1, NYH)] + [other_core]
    for peer in peers:
        pl.semaphore_signal(barrier, inc=1, device_id=peer, device_id_type=MESH)

    def load(src, dst, i):
        copy = pltpu.make_async_copy(src, dst, local_sems.at[i])
        copy.start()
        return copy

    smalls = [
        (owner_hbm, owner_ref),
        (row_hbm, row_ref),
        (positive_hbm, positive),
        (gain_hbm, gain_ref),
        (bias_out_hbm, bias_out_ref),
        (bias_in_hbm, bias_in_ref),
    ]
    small_loads = [load(src, dst, 7 + i) for i, (src, dst) in enumerate(smalls)]
    table_load = load(table_hbm, table, 2)
    queries_load = load(queries_hbm, queries, 3)
    own_tools = load(tools, toolsb.at[c * NYH + yh], 4)
    for copy in small_loads:
        copy.wait()
    gain = gain_ref[...].astype(F32).reshape(1, feat)
    bias_out = bias_out_ref[...].astype(F32).reshape(1, feat)
    bias_in = jnp.pad(bias_in_ref[...].astype(F32).reshape(1, units), ((0, 0), (0, 128 - units)))

    eye = iota((chains, chains), 0) == iota((chains, chains), 1)
    owner_row = owner_ref[...]
    owner = jnp.sum(jnp.where(eye, owner_row.astype(F32), 0.0), axis=1, keepdims=True).astype(I32)
    own_mask = owner == iota((chains, NZ * NP), 1)
    earlier = bits(iota((chains, chains), 1) < iota((chains, chains), 0))
    prior = dot(earlier, bits(own_mask))
    rank = jnp.sum(jnp.where(own_mask, prior, 0.0), axis=1, keepdims=True).astype(I32)
    row_col = jnp.sum(jnp.where(eye, row_ref[...].astype(F32), 0.0), axis=1, keepdims=True)
    lane_of = (owner & (NP - 1)) * CAP + rank
    spread = jnp.where(iota((chains, 128), 1) == lane_of, row_col, 0.0).astype(BF)
    to_z = bits((owner_row >> 3) == iota((16, chains), 0))
    bias_line = jnp.where(iota((16, 128), 0) == NZ, bias_in, 0.0)
    req1[...] = dot(to_z, spread) + bias_line
    rcv1[z] = req1[...]
    pl.semaphore_wait(barrier, len(peers))
    reqs1 = [send(req1, rcv1.at[z], z_peer(o)) for o in range(1, NZ)]

    in_slot, out_slot = wb.at[z, x, 0:units], wb.at[z, x, units : 2 * units]
    y_in = remote(w_in, in_slot, y_flip)
    y_out = remote(w_out, out_slot, y_flip)
    own_in = pltpu.make_async_copy(w_in, in_slot, local_sems.at[5])
    own_out = pltpu.make_async_copy(w_out, out_slot, local_sems.at[6])

    @pl.when(c == yl)
    def _():
        y_in.start()
        y_out.start()
        own_in.start()
        own_out.start()

    @pl.when(c == yl)
    def _():
        own_in.wait()
        own_out.wait()

    @pl.when(c != yl)
    def _():
        y_in.wait_recv()
        y_out.wait_recv()

    def a_part(zz, xx):
        return wb.at[zz, xx, 0:split]

    def b_part(zz, xx):
        return wb.at[zz, xx, split : 2 * units]

    a_x = {NX - o: send(a_part(z, x), a_part(z, x), x_peer(o)) for o in range(1, NX)}
    a_next, a_prev, b_next, b_prev, b_x = {}, {}, {}, {}, {}

    def a_step(k, j):
        xj = lax.rem(x + j, NX)
        if k == 1 and j > 0:
            arrive([a_x[j]])
        if k > 1:
            arrive([a_next[k - 1, j]])
        src = a_part(zb(k - 1), xj)
        a_next[k, j] = send(src, src, z_next)
        if k <= 3:
            if k > 1:
                arrive([a_prev[k - 1, j]])
            src = a_part(zb(1 - k), xj)
            a_prev[k, j] = send(src, src, z_prev)

    def b_cross(k):
        if k:
            arrive([b_next[k] if k > 0 else b_prev[-k]])
        src = b_part(zb(k), x)
        b_x[k, 1] = send(src, src, x_next)
        b_x[k, -1] = send(src, src, x_prev)

    def b_relay(k):
        arrive([b_x[k, 1]])
        src = b_part(zb(k), xb(1))
        b_x[k, 2] = send(src, src, x_next)

    def b_step(k):
        if k > 1:
            arrive([b_next[k - 1]])
        src = b_part(zb(k - 1), x)
        b_next[k] = send(src, src, z_next)
        if k <= 3:
            if k > 1:
                arrive([b_prev[k - 1]])
            src = b_part(zb(1 - k), x)
            b_prev[k] = send(src, src, z_prev)

    b_step(1)
    a_step(1, 0)
    b_cross(0)

    arrive(reqs1)
    for zz in range(NZ):
        tile = rcv1[zz]
        mine = jnp.where(iota((16, 128), 0) == z, tile, 0.0)
        req2[zz : zz + 1, :] = jnp.sum(mine, axis=0, keepdims=True)
        req2[NZ + zz : NZ + zz + 1, :] = tile[NZ : NZ + 1, :]
    rcv2[p] = req2[...]
    reqs2 = [send(req2, rcv2.at[p], p_peer(o)) for o in range(1, NP)]

    b_step(2)
    b_cross(1)
    b_cross(-1)
    for j in range(1, NX):
        a_step(1, j)
    b_relay(0)

    arrive(reqs2)
    table_load.wait()
    asked = jnp.concatenate([rcv2[pp, 0:NZ, :] for pp in range(NP)], axis=0).astype(BF)
    slots = NZ * NP * CAP
    thrice = dot(bits((iota((slots, NZ * NP), 0) >> 2) == iota((slots, NZ * NP), 1)), asked)
    lane_mine = iota((slots, 128), 1) == (iota((slots, 128), 0) & (CAP - 1)) + CAP * p
    wanted = jnp.sum(jnp.where(lane_mine, thrice, 0.0), axis=1, keepdims=True).astype(I32)
    pick = bits(wanted == iota((slots, table.shape[0]), 1))
    rows1, rows2 = [], []
    for h in halves:
        g1b[h] = dot(pick, table[:, cuts[h]]).astype(BF).reshape(g1b.shape[1:])
        rows1.append(spread_out(g1b.at[h], ra.at[h], p, NP, p_peer))

    b_step(3)
    b_cross(2)
    b_cross(-2)
    a_step(2, 0)
    a_step(2, 1)
    a_step(2, 2)
    a_step(2, 3)
    b_relay(1)
    b_relay(-1)

    i0 = iota((slots, slots), 0)
    order1 = ((i0 >> 2) & (NP - 1)) * 32 + (i0 >> 5) * CAP + (i0 & (CAP - 1))
    regroup = bits(order1 == iota((slots, slots), 1))
    for h in halves:
        arrive(rows1[h])
        bb[h] = dot(regroup, ra[h].reshape(slots, half_feat)).astype(BF).reshape(bb.shape[1:])
        rows2.append(spread_out(bb.at[h], fb.at[h], z, NZ, z_peer))
    tool_sends = [send(tools, toolsb.at[c * NYH + yh], y_peer(o)) for o in range(1, NYH)]
    tool_swaps = [send(tools, toolsb.at[c * NYH + yh], other_core)]

    b_step(4)
    b_cross(3)
    b_cross(-3)
    b_relay(2)
    b_relay(-2)
    b_cross(4)
    a_step(3, 0)
    a_step(3, 1)
    b_relay(3)
    b_relay(-3)

    width = NX * units
    bias_rows = jnp.concatenate([rcv2[NYL * xx + c, NZ : 2 * NZ, :] for xx in range(NX)], axis=1)
    line = iota((NX * 128, width), 0)
    lane_to = bits(((line & 127) < units) & (iota((NX * 128, width), 1) == (line >> 7) * units + (line & 127)))
    bias_mat[...] = dot(bias_rows.astype(BF), lane_to)
    queries_load.wait()

    arrive(rows2[0] + rows2[1])
    select = bits(owner * CAP + rank == iota((chains, slots), 1))
    first_rows = [dot(select, fb[h].reshape(slots, half_feat)) for h in halves]
    combined = queries[...].astype(F32) + jnp.concatenate(first_rows, axis=1)
    centred = combined - jnp.mean(combined, axis=1, keepdims=True)
    spread_sq = jnp.mean(centred * centred, axis=1, keepdims=True)
    normed = centred * lax.rsqrt(spread_sq + 1e-05) * gain
    nbuf[c] = normed.astype(BF)
    swap_n = send(nbuf.at[c], nbuf.at[c], other_core)

    a_step(3, 2)
    a_step(3, 3)
    b_relay(4)

    arrive([swap_n])
    both = nbuf[...].reshape(2 * chains, feat)

    def hidden(k):
        if k:
            arrive([(a_next if k > 0 else a_prev)[abs(k), j] for j in range(NX)])
        arrive([b_x[k, -1], b_x[k, 2]])
        zz = zb(k)
        pre = dot_t(both, wb[zz, :, 0:units].reshape(width, feat)) + bias_mat[pl.ds(zz, 1), :]
        term = dot(gelu(pre).astype(BF), wb[zz, :, units : 2 * units].reshape(width, feat)).reshape(pbuf.shape)
        pbuf[...] = term if k == 0 else pbuf[...] + term

    hidden(0)
    for j in range(NX):
        a_step(4, j)
    arrive(tool_sends)
    for o in range(1, NYH):
        slot = toolsb.at[c * NYH + lax.rem(yh + o, NYH)]
        tool_swaps.append(send(slot, slot, other_core))
    for k in (1, -1, 2, -2, 3, -3, 4):
        hidden(k)
    swap_p = send(pbuf.at[1 - c], rbuf, other_core)
    arrive([swap_p])
    updated = (combined + (pbuf[c] + rbuf[...]) + bias_out).astype(BF)
    updb[c] = updated
    swap_u = send(updb.at[c], updb.at[c], other_core)
    updated_out = load(updb.at[c], updated_hbm, 13)

    arrive(tool_swaps)
    own_tools.wait()
    all_tools = toolsb[...].reshape(NC * NYH * tools.shape[0], -1)
    n_tools = all_tools.shape[0]
    half = n_tools // 2
    scores = dot_t(updated, all_tools)
    pos = jnp.sum(jnp.where(eye, positive[...].astype(F32), 0.0), axis=1, keepdims=True).astype(I32)
    pos_col = ((pos >> 6) & 1) * half + (pos >> 7) * 64 + (pos & 63)
    is_pos = iota((chains, n_tools), 1) == pos_col
    top = jnp.max(scores, axis=1, keepdims=True)
    log_total = top + jnp.log(jnp.sum(jnp.exp(scores - top), axis=1, keepdims=True))
    loss = log_total - jnp.sum(jnp.where(is_pos, scores, 0.0), axis=1, keepdims=True)
    grad = (jnp.exp(scores - log_total) - jnp.where(is_pos, 1.0, 0.0)).astype(BF)
    wgb[0] = grad[:, :half]
    wgb[1] = grad[:, half:]
    swap_w = send(wgb.at[1 - c], wga.at[c], other_core)
    wga[c] = wgb[c]

    arrive([swap_u, swap_w])
    i1 = iota((half, half), 0)
    order2 = ((i1 >> 3) & (NYH - 1)) * 64 + (i1 >> 5) * 8 + (i1 & 7)
    grad_t = dot_t(bits(order2 == iota((half, half), 1)), wga[...].reshape(2 * chains, half)).astype(BF)
    stage1, stage2, stage3, stage4 = [], [], [], []
    for h in halves:
        part = dot(grad_t, updb[:, :, cuts[h]].reshape(2 * chains, half_feat))
        s1b[h] = part.astype(BF).reshape(s1b.shape[1:])
        stage1.append(spread_out(s1b.at[h], s1r.at[h], p, NP, p_peer))
    loss_ref[...] = jnp.sum(jnp.where(eye, loss, 0.0), axis=0, keepdims=True)
    qgrad_buf[...] = dot(grad, all_tools)
    qgrad_out = load(qgrad_buf, qgrad_hbm, 14)
    for h in halves:
        arrive(stage1[h])
        s2b[h] = added(s1r.at[h], NP).astype(BF).reshape(s2b.shape[1:])
        stage2.append(spread_out(s2b.at[h], s2r.at[h], yh, NYH, y_peer))
    for h in halves:
        arrive(stage2[h])
        s3r[h, z] = added(s2r.at[h], NYH).astype(BF)
        stage3.append([send(s3r.at[h, z], s3r.at[h, z], z_peer(o)) for o in range(1, NZ)])
    for h in halves:
        arrive(stage3[h])
        s4r[h, p] = (added(s3r.at[h], NZ) * grad_scale).astype(BF)
        stage4.append([send(s4r.at[h, p], s4r.at[h, p], p_peer(o)) for o in range(1, NP)])
    for h in halves:
        arrive(stage4[h])
        tgrad_ref[:, cuts[h]] = s4r[h].astype(F32).reshape(-1, half_feat)
    updated_out.wait()
    qgrad_out.wait()

    for copy in started:
        copy.wait_send()

    @pl.when(c == yl)
    def _():
        y_in.wait_send()
        y_out.wait_send()


def hand_over(*refs):
    held, sems = refs[8:12], refs[12]
    copies_in = [pltpu.make_async_copy(refs[i], held[i], sems.at[i]) for i in range(4)]
    copies_out = [pltpu.make_async_copy(held[i], refs[4 + i], sems.at[4 + i]) for i in range(4)]
    for copy in copies_in:
        copy.start()
    for copy_in, copy_out in zip(copies_in, copies_out):
        copy_in.wait()
        copy_out.start()
    for copy in copies_out:
        copy.wait()


def solution(mesh):
    def local(queries, owner, row, table, gain, w_in, bias_in, w_out, bias_out, tools, positive):
        n, feat = queries.shape
        units = w_in.shape[0]
        block = tools.shape[0]
        scale = (block * mesh.shape["dp"] / (n * mesh.shape["dp"] * mesh.shape["mp"])) ** 0.5
        vmem = pl.BlockSpec(memory_space=pltpu.VMEM)
        hbm = pl.BlockSpec(memory_space=pltpu.HBM)
        slot_rows = NP * CAP
        sub = block // NP
        scratch = [
            pltpu.VMEM((n, feat), BF),
            pltpu.VMEM((1, n), I32),
            pltpu.VMEM((1, n), I32),
            pltpu.VMEM((1, n), I32),
            pltpu.VMEM(table.shape, BF),
            pltpu.VMEM((feat,), BF),
            pltpu.VMEM((feat,), BF),
            pltpu.VMEM((units,), BF),
            pltpu.VMEM((NZ, NX * units), F32),
            pltpu.VMEM((NZ, NX, 2 * units, feat), BF),
            pltpu.VMEM((NC * NYH, block, feat), BF),
            pltpu.VMEM((16, 128), F32),
            pltpu.VMEM((NZ, 16, 128), F32),
            pltpu.VMEM((16, 128), F32),
            pltpu.VMEM((NP, 16, 128), F32),
            pltpu.VMEM((2, NP, slot_rows, feat // 2), BF),
            pltpu.VMEM((2, NP, slot_rows, feat // 2), BF),
            pltpu.VMEM((2, NZ, slot_rows, feat // 2), BF),
            pltpu.VMEM((2, NZ, slot_rows, feat // 2), BF),
            pltpu.VMEM((NC, n, feat), BF),
            pltpu.VMEM((NC, n, feat), F32),
            pltpu.VMEM((n, feat), F32),
            pltpu.VMEM((NC, n, feat), BF),
            pltpu.VMEM((NC, n, NYH * block), BF),
            pltpu.VMEM((NC, n, NYH * block), BF),
            pltpu.VMEM((2, NP, NYH * sub, feat // 2), BF),
            pltpu.VMEM((2, NP, NYH * sub, feat // 2), BF),
            pltpu.VMEM((2, NYH, sub, feat // 2), BF),
            pltpu.VMEM((2, NYH, sub, feat // 2), BF),
            pltpu.VMEM((2, NZ, sub, feat // 2), BF),
            pltpu.VMEM((2, NP, sub, feat // 2), BF),
            pltpu.VMEM((n, feat), F32),
            pltpu.SemaphoreType.DMA((N_SEMS,)),
            pltpu.SemaphoreType.DMA((N_SEMS,)),
            pltpu.SemaphoreType.DMA((15,)),
        ]
        updated, loss, qgrad, tgrad = pl.pallas_call(
            functools.partial(kernel, scale),
            out_shape=(
                jax.ShapeDtypeStruct((n, feat), BF),
                jax.ShapeDtypeStruct((1, n), F32),
                jax.ShapeDtypeStruct((n, feat), F32),
                jax.ShapeDtypeStruct((block, feat), F32),
            ),
            in_specs=[pl.BlockSpec(memory_space=pltpu.HBM)] * 11,
            out_specs=(hbm, vmem, hbm, vmem),
            scratch_shapes=scratch,
            compiler_params=pltpu.CompilerParams(
                collective_id=0, has_side_effects=True, vmem_limit_bytes=63 << 20
            ),
        )(
            queries,
            owner.reshape(1, n),
            row.reshape(1, n),
            positive.reshape(1, n),
            table,
            w_in,
            w_out,
            tools,
            gain,
            bias_out,
            bias_in,
        )
        results = (updated, loss, qgrad, tgrad)
        updated, loss, qgrad, tgrad = pl.pallas_call(
            hand_over,
            out_shape=tuple(jax.ShapeDtypeStruct(r.shape, r.dtype) for r in results),
            in_specs=[hbm] * 4,
            out_specs=(hbm,) * 4,
            scratch_shapes=[pltpu.VMEM(r.shape, r.dtype) for r in results] + [pltpu.SemaphoreType.DMA((8,))],
            compiler_params=pltpu.CompilerParams(vmem_limit_bytes=63 << 20),
        )(*results)
        return updated, loss.reshape(n), qgrad, tgrad

    in_specs = (
        P(("dp", "mp"), None),
        P(("dp", "mp"), None),
        P(("dp", "mp")),
        P("mp", None),
        P(),
        P("mp", None),
        P("mp"),
        P("mp", None),
        P(),
        P("dp", None),
        P(("dp", "mp")),
    )
    out_specs = (P(("dp", "mp"), None), P(("dp", "mp")), P(("dp", "mp"), None), P("dp", None))
    return jax.shard_map(local, mesh=mesh, in_specs=in_specs, out_specs=out_specs, check_vma=False)
```

```python
import functools

import jax
import jax.numpy as jnp
from jax import lax
from jax.experimental import pallas as pl
from jax.experimental.pallas import tpu as pltpu
from jax.sharding import PartitionSpec as P

MESH = pl.DeviceIdType.MESH
BF, F32, I32 = jnp.bfloat16, jnp.float32, jnp.int32
NZ, NX, NYL, NYH, NC = 8, 4, 2, 4, 2
NP = NX * NYL
CAP = 4
N_SEMS = 192


def iota(shape, axis):
    return lax.broadcasted_iota(I32, shape, axis)


def bits(mask):
    return jnp.where(mask, 1.0, 0.0).astype(BF)


def dot(a, b):
    return jnp.dot(a, b, preferred_element_type=F32)


def dot_t(a, b):
    return lax.dot_general(a, b, (((1,), (1,)), ((), ())), preferred_element_type=F32)


def gelu(u):
    return 0.5 * u * (1.0 + jnp.tanh(0.7978845608028654 * (u + 0.044715 * (u * u * u))))


def kernel(
    grad_scale,
    queries_hbm,
    owner_hbm,
    row_hbm,
    positive_hbm,
    table_hbm,
    w_in,
    w_out,
    tools,
    gain_hbm,
    bias_out_hbm,
    bias_in_hbm,
    updated_hbm,
    loss_ref,
    qgrad_hbm,
    tgrad_ref,
    queries,
    owner_ref,
    row_ref,
    positive,
    table,
    gain_ref,
    bias_out_ref,
    bias_in_ref,
    bias_mat,
    wb,
    toolsb,
    req1,
    rcv1,
    req2,
    rcv2,
    g1b,
    ra,
    bb,
    fb,
    nbuf,
    pbuf,
    rbuf,
    updb,
    wgb,
    wga,
    s1b,
    s1r,
    s2b,
    s2r,
    s3r,
    s4r,
    qgrad_buf,
    send_sems,
    recv_sems,
    local_sems,
):
    d, m = lax.axis_index("dp"), lax.axis_index("mp")
    yh, c = lax.div(d, NC), lax.rem(d, NC)
    z, p = lax.div(m, NP), lax.rem(m, NP)
    x, yl = lax.div(p, NYL), lax.rem(p, NYL)
    chains, feat = queries.shape
    units = w_in.shape[0]
    split = 2 * units // 3

    def z_peer(o):
        return {"mp": lax.rem(z + o, NZ) * NP + p}

    def p_peer(o):
        return {"mp": z * NP + lax.rem(p + o, NP)}

    def x_peer(o):
        return {"mp": z * NP + lax.rem(x + o, NX) * NYL + yl}

    def y_peer(o):
        return {"dp": lax.rem(yh + o, NYH) * NC + c}

    other_core = {"dp": yh * NC + (1 - c)}
    y_flip = {"mp": z * NP + x * NYL + (1 - yl)}
    z_next = {"mp": lax.rem(z + 1 + (NZ - 2) * c, NZ) * NP + p}
    z_prev = {"mp": lax.rem(z + (NZ - 1) - (NZ - 2) * c, NZ) * NP + p}
    x_next = {"mp": z * NP + lax.rem(x + 1 + (NX - 2) * c, NX) * NYL + yl}
    x_prev = {"mp": z * NP + lax.rem(x + (NX - 1) - (NX - 2) * c, NX) * NYL + yl}

    def zb(k):
        return lax.rem(z - k + 2 * k * c + NZ, NZ)

    def xb(k):
        return lax.rem(x - k + 2 * k * c + NX, NX)

    count = [0]
    started = []
    arrived = set()

    def remote(src, dst, peer):
        i = count[0]
        count[0] += 1
        return pltpu.make_async_remote_copy(
            src_ref=src,
            dst_ref=dst,
            send_sem=send_sems.at[i],
            recv_sem=recv_sems.at[i],
            device_id=peer,
            device_id_type=MESH,
        )

    def send(src, dst, peer):
        copy = remote(src, dst, peer)
        copy.start()
        started.append(copy)
        return copy

    def arrive(copies):
        for copy in copies:
            if id(copy) not in arrived:
                arrived.add(id(copy))
                copy.wait_recv()

    halves = range(2)
    half_feat = feat // 2
    cuts = [slice(h * half_feat, (h + 1) * half_feat) for h in halves]

    def spread_out(buf, got, me, count, peer_of):
        got[me] = buf[me]
        return [send(buf.at[lax.rem(me + o, count)], got.at[me], peer_of(o)) for o in range(1, count)]

    def added(got, count):
        total = got[0].astype(F32)
        for i in range(1, count):
            total = total + got[i].astype(F32)
        return total

    barrier = pltpu.get_barrier_semaphore()
    peers = [z_peer(o) for o in range(1, NZ)] + [p_peer(o) for o in range(1, NP)]
    peers += [y_peer(o) for o in range(1, NYH)] + [other_core]
    for peer in peers:
        pl.semaphore_signal(barrier, inc=1, device_id=peer, device_id_type=MESH)

    def load(src, dst, i):
        copy = pltpu.make_async_copy(src, dst, local_sems.at[i])
        copy.start()
        return copy

    smalls = [
        (owner_hbm, owner_ref),
        (row_hbm, row_ref),
        (positive_hbm, positive),
        (gain_hbm, gain_ref),
        (bias_out_hbm, bias_out_ref),
        (bias_in_hbm, bias_in_ref),
    ]
    small_loads = [load(src, dst, 7 + i) for i, (src, dst) in enumerate(smalls)]
    table_load = load(table_hbm, table, 2)
    queries_load = load(queries_hbm, queries, 3)
    own_tools = load(tools, toolsb.at[c * NYH + yh], 4)
    for copy in small_loads:
        copy.wait()
    gain = gain_ref[...].astype(F32).reshape(1, feat)
    bias_out = bias_out_ref[...].astype(F32).reshape(1, feat)
    bias_in = jnp.pad(bias_in_ref[...].astype(F32).reshape(1, units), ((0, 0), (0, 128 - units)))

    eye = iota((chains, chains), 0) == iota((chains, chains), 1)
    owner_row = owner_ref[...]
    owner = jnp.sum(jnp.where(eye, owner_row.astype(F32), 0.0), axis=1, keepdims=True).astype(I32)
    own_mask = owner == iota((chains, NZ * NP), 1)
    earlier = bits(iota((chains, chains), 1) < iota((chains, chains), 0))
    prior = dot(earlier, bits(own_mask))
    rank = jnp.sum(jnp.where(own_mask, prior, 0.0), axis=1, keepdims=True).astype(I32)
    row_col = jnp.sum(jnp.where(eye, row_ref[...].astype(F32), 0.0), axis=1, keepdims=True)
    lane_of = (owner & (NP - 1)) * CAP + rank
    spread = jnp.where(iota((chains, 128), 1) == lane_of, row_col, 0.0).astype(BF)
    to_z = bits((owner_row >> 3) == iota((16, chains), 0))
    bias_line = jnp.where(iota((16, 128), 0) == NZ, bias_in, 0.0)
    req1[...] = dot(to_z, spread) + bias_line
    rcv1[z] = req1[...]
    pl.semaphore_wait(barrier, len(peers))
    reqs1 = [send(req1, rcv1.at[z], z_peer(o)) for o in range(1, NZ)]

    in_slot, out_slot = wb.at[z, x, 0:units], wb.at[z, x, units : 2 * units]
    y_in = remote(w_in, in_slot, y_flip)
    y_out = remote(w_out, out_slot, y_flip)
    own_in = pltpu.make_async_copy(w_in, in_slot, local_sems.at[5])
    own_out = pltpu.make_async_copy(w_out, out_slot, local_sems.at[6])

    @pl.when(c == yl)
    def _():
        y_in.start()
        y_out.start()
        own_in.start()
        own_out.start()

    @pl.when(c == yl)
    def _():
        own_in.wait()
        own_out.wait()

    @pl.when(c != yl)
    def _():
        y_in.wait_recv()
        y_out.wait_recv()

    def a_part(zz, xx):
        return wb.at[zz, xx, 0:split]

    def b_part(zz, xx):
        return wb.at[zz, xx, split : 2 * units]

    a_x = {NX - o: send(a_part(z, x), a_part(z, x), x_peer(o)) for o in range(1, NX)}
    a_next, a_prev, b_next, b_prev, b_x = {}, {}, {}, {}, {}

    def a_step(k, j):
        xj = lax.rem(x + j, NX)
        if k == 1 and j > 0:
            arrive([a_x[j]])
        if k > 1:
            arrive([a_next[k - 1, j]])
        src = a_part(zb(k - 1), xj)
        a_next[k, j] = send(src, src, z_next)
        if k <= 3:
            if k > 1:
                arrive([a_prev[k - 1, j]])
            src = a_part(zb(1 - k), xj)
            a_prev[k, j] = send(src, src, z_prev)

    def b_cross(k):
        if k:
            arrive([b_next[k] if k > 0 else b_prev[-k]])
        src = b_part(zb(k), x)
        b_x[k, 1] = send(src, src, x_next)
        b_x[k, -1] = send(src, src, x_prev)

    def b_relay(k):
        arrive([b_x[k, 1]])
        src = b_part(zb(k), xb(1))
        b_x[k, 2] = send(src, src, x_next)

    def b_step(k):
        if k > 1:
            arrive([b_next[k - 1]])
        src = b_part(zb(k - 1), x)
        b_next[k] = send(src, src, z_next)
        if k <= 3:
            if k > 1:
                arrive([b_prev[k - 1]])
            src = b_part(zb(1 - k), x)
            b_prev[k] = send(src, src, z_prev)

    b_step(1)
    a_step(1, 0)
    b_cross(0)

    arrive(reqs1)
    for zz in range(NZ):
        tile = rcv1[zz]
        mine = jnp.where(iota((16, 128), 0) == z, tile, 0.0)
        req2[zz : zz + 1, :] = jnp.sum(mine, axis=0, keepdims=True)
        req2[NZ + zz : NZ + zz + 1, :] = tile[NZ : NZ + 1, :]
    rcv2[p] = req2[...]
    reqs2 = [send(req2, rcv2.at[p], p_peer(o)) for o in range(1, NP)]
    tool_sends = [send(tools, toolsb.at[c * NYH + yh], y_peer(o)) for o in range(1, NYH)]
    tool_swaps = [send(tools, toolsb.at[c * NYH + yh], other_core)]

    b_step(2)
    b_cross(1)
    b_cross(-1)
    for j in range(1, NX):
        a_step(1, j)
    b_relay(0)

    arrive(reqs2)
    table_load.wait()
    asked = jnp.concatenate([rcv2[pp, 0:NZ, :] for pp in range(NP)], axis=0).astype(BF)
    slots = NZ * NP * CAP
    thrice = dot(bits((iota((slots, NZ * NP), 0) >> 2) == iota((slots, NZ * NP), 1)), asked)
    lane_mine = iota((slots, 128), 1) == (iota((slots, 128), 0) & (CAP - 1)) + CAP * p
    wanted = jnp.sum(jnp.where(lane_mine, thrice, 0.0), axis=1, keepdims=True).astype(I32)
    pick = bits(wanted == iota((slots, table.shape[0]), 1))
    rows1, rows2 = [], []
    for h in halves:
        g1b[h] = dot(pick, table[:, cuts[h]]).astype(BF).reshape(g1b.shape[1:])
        rows1.append(spread_out(g1b.at[h], ra.at[h], p, NP, p_peer))

    b_step(3)
    b_cross(2)
    b_cross(-2)
    a_step(2, 0)
    a_step(2, 1)
    a_step(2, 2)
    a_step(2, 3)
    b_relay(1)
    b_relay(-1)

    i0 = iota((slots, slots), 0)
    order1 = ((i0 >> 2) & (NP - 1)) * 32 + (i0 >> 5) * CAP + (i0 & (CAP - 1))
    regroup = bits(order1 == iota((slots, slots), 1))
    for h in halves:
        arrive(rows1[h])
        bb[h] = dot(regroup, ra[h].reshape(slots, half_feat)).astype(BF).reshape(bb.shape[1:])
        rows2.append(spread_out(bb.at[h], fb.at[h], z, NZ, z_peer))

    b_step(4)
    b_cross(3)
    b_cross(-3)
    b_relay(2)
    b_relay(-2)
    b_cross(4)
    a_step(3, 0)
    a_step(3, 1)
    b_relay(3)
    b_relay(-3)

    width = NX * units
    bias_rows = jnp.concatenate([rcv2[NYL * xx + c, NZ : 2 * NZ, :] for xx in range(NX)], axis=1)
    line = iota((NX * 128, width), 0)
    lane_to = bits(((line & 127) < units) & (iota((NX * 128, width), 1) == (line >> 7) * units + (line & 127)))
    bias_mat[...] = dot(bias_rows.astype(BF), lane_to)
    queries_load.wait()

    arrive(rows2[0] + rows2[1])
    select = bits(owner * CAP + rank == iota((chains, slots), 1))
    first_rows = [dot(select, fb[h].reshape(slots, half_feat)) for h in halves]
    combined = queries[...].astype(F32) + jnp.concatenate(first_rows, axis=1)
    centred = combined - jnp.mean(combined, axis=1, keepdims=True)
    spread_sq = jnp.mean(centred * centred, axis=1, keepdims=True)
    normed = centred * lax.rsqrt(spread_sq + 1e-05) * gain
    nbuf[c] = normed.astype(BF)
    swap_n = send(nbuf.at[c], nbuf.at[c], other_core)

    a_step(3, 2)
    a_step(3, 3)
    b_relay(4)

    arrive([swap_n])
    both = nbuf[...].reshape(2 * chains, feat)

    def hidden(k):
        if k:
            arrive([(a_next if k > 0 else a_prev)[abs(k), j] for j in range(NX)])
        arrive([b_x[k, -1], b_x[k, 2]])
        zz = zb(k)
        pre = dot_t(both, wb[zz, :, 0:units].reshape(width, feat)) + bias_mat[pl.ds(zz, 1), :]
        term = dot(gelu(pre).astype(BF), wb[zz, :, units : 2 * units].reshape(width, feat)).reshape(pbuf.shape)
        pbuf[...] = term if k == 0 else pbuf[...] + term

    hidden(0)
    for j in range(NX):
        a_step(4, j)
    arrive(tool_sends)
    for o in range(1, NYH):
        slot = toolsb.at[c * NYH + lax.rem(yh + o, NYH)]
        tool_swaps.append(send(slot, slot, other_core))
    for k in (1, -1, 2, -2, 3, -3, 4):
        hidden(k)
    swap_p = send(pbuf.at[1 - c], rbuf, other_core)
    arrive([swap_p])
    updated = (combined + (pbuf[c] + rbuf[...]) + bias_out).astype(BF)
    updb[c] = updated
    swap_u = send(updb.at[c], updb.at[c], other_core)
    updated_out = load(updb.at[c], updated_hbm, 13)

    arrive(tool_swaps)
    own_tools.wait()
    all_tools = toolsb[...].reshape(NC * NYH * tools.shape[0], -1)
    n_tools = all_tools.shape[0]
    half = n_tools // 2
    scores = dot_t(updated, all_tools)
    pos = jnp.sum(jnp.where(eye, positive[...].astype(F32), 0.0), axis=1, keepdims=True).astype(I32)
    pos_col = ((pos >> 6) & 1) * half + (pos >> 7) * 64 + (pos & 63)
    is_pos = iota((chains, n_tools), 1) == pos_col
    top = jnp.max(scores, axis=1, keepdims=True)
    log_total = top + jnp.log(jnp.sum(jnp.exp(scores - top), axis=1, keepdims=True))
    loss = log_total - jnp.sum(jnp.where(is_pos, scores, 0.0), axis=1, keepdims=True)
    grad = (jnp.exp(scores - log_total) - jnp.where(is_pos, 1.0, 0.0)).astype(BF)
    wgb[0] = grad[:, :half]
    wgb[1] = grad[:, half:]
    swap_w = send(wgb.at[1 - c], wga.at[c], other_core)
    wga[c] = wgb[c]

    arrive([swap_u, swap_w])
    i1 = iota((half, half), 0)
    order2 = ((i1 >> 3) & (NYH - 1)) * 64 + (i1 >> 5) * 8 + (i1 & 7)
    grad_t = dot_t(bits(order2 == iota((half, half), 1)), wga[...].reshape(2 * chains, half)).astype(BF)
    stage1, stage2, stage3, stage4 = [], [], [], []
    for h in halves:
        part = dot(grad_t, updb[:, :, cuts[h]].reshape(2 * chains, half_feat))
        s1b[h] = part.astype(BF).reshape(s1b.shape[1:])
        stage1.append(spread_out(s1b.at[h], s1r.at[h], p, NP, p_peer))
    loss_ref[...] = jnp.sum(jnp.where(eye, loss, 0.0), axis=0, keepdims=True)
    qgrad_buf[...] = dot(grad, all_tools)
    qgrad_out = load(qgrad_buf, qgrad_hbm, 14)
    for h in halves:
        arrive(stage1[h])
        s2b[h] = added(s1r.at[h], NP).astype(BF).reshape(s2b.shape[1:])
        stage2.append(spread_out(s2b.at[h], s2r.at[h], yh, NYH, y_peer))
    for h in halves:
        arrive(stage2[h])
        s3r[h, z] = added(s2r.at[h], NYH).astype(BF)
        stage3.append([send(s3r.at[h, z], s3r.at[h, z], z_peer(o)) for o in range(1, NZ)])
    for h in halves:
        arrive(stage3[h])
        s4r[h, p] = (added(s3r.at[h], NZ) * grad_scale).astype(BF)
        stage4.append([send(s4r.at[h, p], s4r.at[h, p], p_peer(o)) for o in range(1, NP)])
    for h in halves:
        arrive(stage4[h])
        tgrad_ref[:, cuts[h]] = s4r[h].astype(F32).reshape(-1, half_feat)
    updated_out.wait()
    qgrad_out.wait()

    for copy in started:
        copy.wait_send()

    @pl.when(c == yl)
    def _():
        y_in.wait_send()
        y_out.wait_send()


def hand_over(*refs):
    held, sems = refs[8:12], refs[12]
    copies_in = [pltpu.make_async_copy(refs[i], held[i], sems.at[i]) for i in range(4)]
    copies_out = [pltpu.make_async_copy(held[i], refs[4 + i], sems.at[4 + i]) for i in range(4)]
    for copy in copies_in:
        copy.start()
    for copy_in, copy_out in zip(copies_in, copies_out):
        copy_in.wait()
        copy_out.start()
    for copy in copies_out:
        copy.wait()


def solution(mesh):
    def local(queries, owner, row, table, gain, w_in, bias_in, w_out, bias_out, tools, positive):
        n, feat = queries.shape
        units = w_in.shape[0]
        block = tools.shape[0]
        scale = (block * mesh.shape["dp"] / (n * mesh.shape["dp"] * mesh.shape["mp"])) ** 0.5
        vmem = pl.BlockSpec(memory_space=pltpu.VMEM)
        hbm = pl.BlockSpec(memory_space=pltpu.HBM)
        slot_rows = NP * CAP
        sub = block // NP
        scratch = [
            pltpu.VMEM((n, feat), BF),
            pltpu.VMEM((1, n), I32),
            pltpu.VMEM((1, n), I32),
            pltpu.VMEM((1, n), I32),
            pltpu.VMEM(table.shape, BF),
            pltpu.VMEM((feat,), BF),
            pltpu.VMEM((feat,), BF),
            pltpu.VMEM((units,), BF),
            pltpu.VMEM((NZ, NX * units), F32),
            pltpu.VMEM((NZ, NX, 2 * units, feat), BF),
            pltpu.VMEM((NC * NYH, block, feat), BF),
            pltpu.VMEM((16, 128), F32),
            pltpu.VMEM((NZ, 16, 128), F32),
            pltpu.VMEM((16, 128), F32),
            pltpu.VMEM((NP, 16, 128), F32),
            pltpu.VMEM((2, NP, slot_rows, feat // 2), BF),
            pltpu.VMEM((2, NP, slot_rows, feat // 2), BF),
            pltpu.VMEM((2, NZ, slot_rows, feat // 2), BF),
            pltpu.VMEM((2, NZ, slot_rows, feat // 2), BF),
            pltpu.VMEM((NC, n, feat), BF),
            pltpu.VMEM((NC, n, feat), F32),
            pltpu.VMEM((n, feat), F32),
            pltpu.VMEM((NC, n, feat), BF),
            pltpu.VMEM((NC, n, NYH * block), BF),
            pltpu.VMEM((NC, n, NYH * block), BF),
            pltpu.VMEM((2, NP, NYH * sub, feat // 2), BF),
            pltpu.VMEM((2, NP, NYH * sub, feat // 2), BF),
            pltpu.VMEM((2, NYH, sub, feat // 2), BF),
            pltpu.VMEM((2, NYH, sub, feat // 2), BF),
            pltpu.VMEM((2, NZ, sub, feat // 2), BF),
            pltpu.VMEM((2, NP, sub, feat // 2), BF),
            pltpu.VMEM((n, feat), F32),
            pltpu.SemaphoreType.DMA((N_SEMS,)),
            pltpu.SemaphoreType.DMA((N_SEMS,)),
            pltpu.SemaphoreType.DMA((15,)),
        ]
        updated, loss, qgrad, tgrad = pl.pallas_call(
            functools.partial(kernel, scale),
            out_shape=(
                jax.ShapeDtypeStruct((n, feat), BF),
                jax.ShapeDtypeStruct((1, n), F32),
                jax.ShapeDtypeStruct((n, feat), F32),
                jax.ShapeDtypeStruct((block, feat), F32),
            ),
            in_specs=[pl.BlockSpec(memory_space=pltpu.HBM)] * 11,
            out_specs=(hbm, vmem, hbm, vmem),
            scratch_shapes=scratch,
            compiler_params=pltpu.CompilerParams(
                collective_id=0, has_side_effects=True, vmem_limit_bytes=63 << 20
            ),
        )(
            queries,
            owner.reshape(1, n),
            row.reshape(1, n),
            positive.reshape(1, n),
            table,
            w_in,
            w_out,
            tools,
            gain,
            bias_out,
            bias_in,
        )
        results = (updated, loss, qgrad, tgrad)
        updated, loss, qgrad, tgrad = pl.pallas_call(
            hand_over,
            out_shape=tuple(jax.ShapeDtypeStruct(r.shape, r.dtype) for r in results),
            in_specs=[hbm] * 4,
            out_specs=(hbm,) * 4,
            scratch_shapes=[pltpu.VMEM(r.shape, r.dtype) for r in results] + [pltpu.SemaphoreType.DMA((8,))],
            compiler_params=pltpu.CompilerParams(vmem_limit_bytes=63 << 20),
        )(*results)
        return updated, loss.reshape(n), qgrad, tgrad

    in_specs = (
        P(("dp", "mp"), None),
        P(("dp", "mp"), None),
        P(("dp", "mp")),
        P("mp", None),
        P(),
        P("mp", None),
        P("mp"),
        P("mp", None),
        P(),
        P("dp", None),
        P(("dp", "mp")),
    )
    out_specs = (P(("dp", "mp"), None), P(("dp", "mp")), P(("dp", "mp"), None), P("dp", None))
    return jax.shard_map(local, mesh=mesh, in_specs=in_specs, out_specs=out_specs, check_vma=False)
```
